128 devices in a mesh: stream: 32 (over x, y, core), radial: 4 (over z).
Axes of the slice: x: 4, y: 4, z: 4, core: 2. Of those that a mesh axis runs over, the one named last changes fastest.
Arguments:
- right_side: float32 [5, 4, 512, 64, 128], P(None, None, 'stream', 'radial'), may hold values from -18 to 18
- diag_block: float32 [5, 5, 512, 64, 128], P(None, None, 'stream', 'radial'), may hold values from -1.5 to 9.5
- face_coef: float32 [6, 512, 64, 128], P(None, 'stream', 'radial'), may hold values from 0.5 to 1.5
- jacobians: float32 [6, 5, 5], replicated, may hold values from -2.4 to 2.4
Outputs:
- basis_q: float32 [5, 16, 512, 64, 128], P(None, None, 'stream', 'radial')
- r_factor: float32 [16, 16], replicated
The draws below stay inside these ranges and needn't reach their ends.
All inputs are finite; a program needn't handle non-finite values.
Results may differ from the reference program's by a relative error of at most 0.00023.
Values sent between devices are 32-bit elements; how exact they have to be, the bound alone decides.
A program may use at most 192 MiB of HBM per device.

```python
import math
import jax
import jax.numpy as jnp
from jax import lax

NV = 5
NRHS = 4
POWERS = 3
NT = 128
NCOL = 16
NS = 512
NR = 64


def draw_right_side(key, part):
    ramp = 1.0 + 2.0 * jnp.arange(NS, dtype=jnp.float32) / max(NS - 1, 1)
    values = jnp.clip(jax.random.normal(key, (NV, NRHS, NS, NR, NT), jnp.float32), -6.0, 6.0)
    return values * ramp[None, None, :, None, None]


def draw_diag_block(key, part):
    first, second = jax.random.split(key)
    diagonal = jnp.exp(jax.random.uniform(first, (NV, NS, NR, NT), jnp.float32, math.log(4.0), math.log(8.0)))
    offdiag = jnp.clip(0.3 * jax.random.normal(second, (NV, NV, NS, NR, NT), jnp.float32), -1.5, 1.5)
    identity = jnp.eye(NV, dtype=jnp.float32)[:, :, None, None, None]
    return offdiag + identity * diagonal[:, None]


def block_scale(key, dims, pieces, low, largest):
    def one(position, shards_of):
        steps = jax.random.uniform(jax.random.fold_in(jax.random.fold_in(key, 6), position), (shards_of,), jnp.float32, low / len(pieces), largest / len(pieces))
        return jnp.repeat(jnp.exp(steps), dims[position] // shards_of).reshape((-1,) + (1,) * (len(dims) - position - 1))

    factor_of = one(*pieces[0])
    for cut in pieces[1:]:
        factor_of = factor_of * one(*cut)
    return factor_of


def noise(rng, shape, scale, bound, kind=jnp.bfloat16):
    values = scale * jax.random.normal(rng, shape, jnp.float32)
    return jnp.clip(values, min=-bound, max=bound).astype(kind)


def setup_inputs(seed: int = 0) -> dict:
    keys = jax.random.split(jax.random.key(seed), 5)
    right_side = draw_right_side(jax.random.fold_in(keys[4], 71), 0)
    diag_block = draw_diag_block(jax.random.fold_in(keys[4], 71), 0)
    face_coef = jnp.clip(0.5 + 1.0 * jax.random.uniform(keys[2], (6, NS, NR, NT), jnp.float32) ** block_scale(keys[2], (6, NS, NR, NT), ((1, 32), (2, 4)), -0.2, 0.2), 0.5, 1.5)
    jacobians = noise(keys[3], (6, NV, NV), 0.4, 2.4, jnp.float32)
    return dict(right_side=right_side, diag_block=diag_block, face_coef=face_coef, jacobians=jacobians)


shift_value = 6.0

def operate(padded, blocks, face_vals, jacobians):
    centre = padded[:, :, 1:-1, 1:-1]
    result = -shift_value * centre
    for column in range(centre.shape[0]):
        result = result + blocks[:, column][:, None] * centre[column][None]
    beside_list = (padded[:, :, :-2, 1:-1], padded[:, :, 2:, 1:-1], padded[:, :, 1:-1, :-2], padded[:, :, 1:-1, 2:], jnp.roll(centre, 1, axis=4), jnp.roll(centre, -1, axis=4))
    for direction in range(6):
        coupled = jnp.einsum('ab,brxyz->arxyz', jacobians[direction], beside_list[direction], precision=lax.Precision.HIGHEST)
        result = result - face_vals[direction][None, None] * coupled
    return result

def unit_columns(vector):
    totals = lax.optimization_barrier(jnp.sum(vector * vector, axis=(0, 2, 3, 4)))
    return vector / jnp.sqrt(totals)[None, :, None, None, None]

def upper_factor(gram_sums):
    order_size = gram_sums.shape[0]
    positions = jnp.arange(order_size)
    factor_rows = []
    for row_number in range(order_size):
        pending = gram_sums[row_number]
        for prior_row in range(row_number):
            pending = pending - factor_rows[prior_row][row_number] * factor_rows[prior_row]
        pivot_root = jnp.sqrt(pending[row_number])
        factor_rows.append(jnp.where(positions >= row_number, pending / pivot_root, jnp.zeros_like(pending)))
    return jnp.stack(factor_rows)

def upper_inverse(factor):
    order_size = factor.shape[0]
    identity = jnp.eye(order_size, dtype=factor.dtype)
    solved = [None] * order_size
    for row_number in reversed(range(order_size)):
        pending = identity[row_number]
        for later_row in range(row_number + 1, order_size):
            pending = pending - factor[row_number, later_row] * solved[later_row]
        solved[row_number] = pending / factor[row_number, row_number]
    return jnp.stack(solved)

def reference(right_side, diag_block, face_coef, jacobians):
    current = unit_columns(right_side)
    columns = [current]
    for power_k in range(POWERS):
        padded = jnp.pad(current, ((0, 0), (0, 0), (1, 1), (1, 1), (0, 0)))
        current = unit_columns(operate(padded, diag_block, face_coef, jacobians))
        columns.append(current)
    basis_cols = jnp.stack(columns, axis=1).reshape(NV, NCOL, NS, NR, NT)
    gram_sums = jnp.einsum('acxyz,adxyz->cd', basis_cols, basis_cols, precision=lax.Precision.HIGHEST)
    r_factor = upper_factor(gram_sums)
    inverse = upper_inverse(r_factor)
    basis_q = jnp.einsum('aixyz,ij->ajxyz', basis_cols, inverse, precision=lax.Precision.HIGHEST)
    return (basis_q, r_factor)
```

```python
import functools

import jax
import jax.numpy as jnp
from jax import lax
from jax.experimental import pallas as pl
from jax.experimental.pallas import tpu as pltpu
from jax.sharding import PartitionSpec as P

NV = 5
NRHS = 4
POWERS = 3
NCOL = 16
LS = 16
LR = 16
NT = 128
ROWS = LS * LR
SHIFT = 6.0
BLK = NV * LR
KDIM = 256
DIRS = ((0, 0), (1, 0), (2, -1), (3, 1), (4, 0), (5, 0), (2, 0), (3, 0))
RAISE = 2.0**24
MESH = pl.DeviceIdType.MESH
HIGH = lax.Precision.HIGHEST


def build_operator(jac_ref, w_ref):
    col = lax.broadcasted_iota(jnp.int32, (LR, KDIM), 1)
    row = lax.broadcasted_iota(jnp.int32, (LR, KDIM), 0)
    part = col // BLK
    var = (col % BLK) // LR
    cell = col % LR
    masks = {}
    for offset in (-1, 0, 1):
        hit = (cell == row + offset) & (part < 3)
        masks[offset] = [
            jnp.where(hit & (var == b), 1.0, 0.0).astype(jnp.float32) for b in range(NV)
        ]
    for block, (direction, offset) in enumerate(DIRS):
        for a in range(NV):
            total = jac_ref[direction, a, 0] * masks[offset][0]
            for b in range(1, NV):
                total = total + jac_ref[direction, a, b] * masks[offset][b]
            head = total.astype(jnp.bfloat16).astype(jnp.float32)
            mixed = jnp.where(part == 1, total - head, head)
            start = block * BLK + a * LR
            w_ref[start : start + LR, :] = mixed.astype(jnp.bfloat16)


def split_fields(values, x_ref):
    head = values.astype(jnp.bfloat16)
    tail = (values - head.astype(jnp.float32)).astype(jnp.bfloat16)
    for r in range(NRHS):
        lanes = slice(r * NT, (r + 1) * NT)
        head_r = head[:, r].reshape(BLK, NT)
        x_ref[0:BLK, lanes] = head_r
        x_ref[BLK : 2 * BLK, lanes] = head_r
        x_ref[2 * BLK : 3 * BLK, lanes] = tail[:, r].reshape(BLK, NT)


def piece(product, block, r):
    return product[block * BLK : (block + 1) * BLK, r * NT : (r + 1) * NT].reshape(NV, LR, NT)


def apply_inner(source, target, diag_ref, face_ref, w_ref, x_ref, q_ref, scale):
    target[:, :, 0:LR, :] = jnp.zeros((NV, NRHS, LR, NT), jnp.float32)
    target[:, :, ROWS : ROWS + LR, :] = jnp.zeros((NV, NRHS, LR, NT), jnp.float32)

    def step(s, carry):
        here = pl.ds(pl.multiple_of(s * LR, LR), LR)
        after = pl.ds(pl.multiple_of((s + 1) * LR, LR), LR)
        before = pl.ds(pl.multiple_of(((s + LS) % (LS + 1)) * LR, LR), LR)
        face_after = pl.ds(pl.multiple_of(jnp.minimum(s + 1, LS - 1) * LR, LR), LR)
        face_before = pl.ds(pl.multiple_of(jnp.maximum(s - 1, 0) * LR, LR), LR)
        values = source[:, :, here, :]
        split_fields(values, x_ref)
        q_ref[...] = jnp.dot(w_ref[0 : 6 * BLK, :], x_ref[...], preferred_element_type=jnp.float32)
        f0 = face_ref[0, face_after, :] * scale
        f1 = face_ref[1, face_before, :] * scale
        f2, f3, f4, f5 = (face_ref[d, here, :] for d in range(2, 6))
        for r in range(NRHS):
            mine = values[:, r]
            total = -SHIFT * mine
            for b in range(NV):
                total = total + diag_ref[:, b, here, :] * mine[b]
            total = total - f2 * piece(q_ref, 2, r)
            total = total - f3 * piece(q_ref, 3, r)
            total = total - f4 * pltpu.roll(piece(q_ref, 4, r), 1, 2)
            total = total - f5 * pltpu.roll(piece(q_ref, 5, r), NT - 1, 2)
            if scale != 1.0:
                total = total * scale
            target[:, r, here, :] = target[:, r, here, :] + total
            target[:, r, after, :] = -(f0 * piece(q_ref, 0, r))
            target[:, r, before, :] = target[:, r, before, :] - f1 * piece(q_ref, 1, r)
        return carry

    lax.fori_loop(0, LS, step, 0)


def add_halo(target, face_ref, w_ref, x_ref, slabs, edges, rows_ref, scale):
    for side in range(2):
        start = 0 if side == 0 else ROWS - LR
        split_fields(slabs[side], x_ref)
        product = jnp.dot(
            w_ref[side * BLK : (side + 1) * BLK, :], x_ref[...], preferred_element_type=jnp.float32
        )
        weight = face_ref[side, start : start + LR, :] * scale
        for r in range(NRHS):
            target[:, r, start : start + LR, :] = target[
                :, r, start : start + LR, :
            ] - weight * piece(product, 0, r)
    for side in range(2):
        rows = pl.ds(0 if side == 0 else LR - 1, LS, stride=LR)
        split_fields(edges[side], x_ref)
        product = jnp.dot(
            w_ref[(6 + side) * BLK : (7 + side) * BLK, :],
            x_ref[...],
            preferred_element_type=jnp.float32,
        )
        weight = face_ref[2 + side, rows, :] * scale
        for a in range(NV):
            for r in range(NRHS):
                fresh = target[a, r, rows, :] - weight * (
                    product[a * LR : (a + 1) * LR, r * NT : (r + 1) * NT]
                )
                target[a, r, rows, :] = fresh
                if rows_ref is not None:
                    rows_ref[side, a, r] = fresh


def local_gram(y_ref, m_ref):
    m_ref[...] = jnp.zeros((ROWS, ROWS), jnp.float32)

    def step(s, carry):
        here = pl.ds(pl.multiple_of(s * LR, LR), LR)
        left = []
        right = []
        for a in range(NV):
            values = jnp.concatenate(
                [y_ref[k, a, :, here, :].reshape(NRHS * LR, NT) for k in range(POWERS + 1)], axis=0
            )
            head = values.astype(jnp.bfloat16)
            tail = (2.0 * (values - head.astype(jnp.float32))).astype(jnp.bfloat16)
            left += [head, tail]
            right += [head, head]
        m_ref[...] += lax.dot_general(
            jnp.concatenate(left, axis=1),
            jnp.concatenate(right, axis=1),
            (((1,), (1,)), ((), ())),
            preferred_element_type=jnp.float32,
        )
        return carry

    lax.fori_loop(0, LS, step, 0)
    row = lax.broadcasted_iota(jnp.int32, (ROWS, ROWS), 0)
    col = lax.broadcasted_iota(jnp.int32, (ROWS, ROWS), 1)
    kept = jnp.where(row % LR == col % LR, m_ref[...], 0.0)
    pick_row = lax.broadcasted_iota(jnp.int32, (NCOL, ROWS), 0)
    pick_col = lax.broadcasted_iota(jnp.int32, (NCOL, ROWS), 1)
    pick = jnp.where(pick_col // LR == pick_row, 1.0, 0.0).astype(jnp.float32)
    wide_row = lax.broadcasted_iota(jnp.int32, (NT, ROWS), 0)
    wide_col = lax.broadcasted_iota(jnp.int32, (NT, ROWS), 1)
    wide = jnp.where(wide_col // LR == wide_row, 1.0, 0.0).astype(jnp.float32)
    half = jnp.dot(pick, kept, precision=HIGH, preferred_element_type=jnp.float32)
    return lax.dot_general(
        half, wide, (((1,), (1,)), ((), ())), precision=HIGH, preferred_element_type=jnp.float32
    )


def krylov_kernel(
    n_stream,
    n_radial,
    right_hbm,
    diag_hbm,
    face_hbm,
    jac_ref,
    y_hbm,
    gram_ref,
    y_ref,
    diag_ref,
    face_ref,
    w_ref,
    x_ref,
    q_ref,
    slab_ref,
    edge_ref,
    pack_ref,
    m_ref,
    first_ref,
    second_ref,
    load_sem,
    out_sem,
    halo_send,
    halo_recv,
    first_send,
    first_recv,
    second_send,
    second_recv,
):
    si = lax.axis_index("stream")
    ri = lax.axis_index("radial")
    core = si % 2
    chip = si // 2
    n_first = 2 * n_radial
    n_second = n_stream // 2
    me_first = ri * 2 + core

    def first_peer(offset):
        other = (me_first + offset) % n_first
        return (chip * 2 + other % 2, other // 2)

    def second_peer(offset):
        return (((chip + offset) % n_second) * 2 + core, ri)

    loads = [
        pltpu.make_async_copy(right_hbm, y_ref.at[0, :, :, pl.ds(0, ROWS), :], load_sem.at[0]),
        pltpu.make_async_copy(face_hbm, face_ref, load_sem.at[1]),
        pltpu.make_async_copy(diag_hbm, diag_ref, load_sem.at[2]),
    ]
    for load in loads:
        load.start()

    barrier = pltpu.get_barrier_semaphore()
    for offset in range(1, n_first):
        pl.semaphore_signal(barrier, inc=1, device_id=first_peer(offset), device_id_type=MESH)
    for offset in range(1, n_second):
        pl.semaphore_signal(barrier, inc=1, device_id=second_peer(offset), device_id_type=MESH)
    peers = ((si + 1, ri), (si - 1, ri), (si, ri + 1), (si, ri - 1))
    present = (si < n_stream - 1, si > 0, ri < n_radial - 1, ri > 0)
    source_of = (1, 0, 3, 2)
    for j in range(4):

        @pl.when(present[j])
        def _(j=j):
            pl.semaphore_signal(barrier, inc=1, device_id=peers[j], device_id_type=MESH)

    x_ref[3 * BLK :, :] = jnp.zeros((KDIM - 3 * BLK, NRHS * NT), jnp.bfloat16)
    build_operator(jac_ref, w_ref)
    for side in range(2):

        @pl.when(jnp.logical_not(present[1 - side]))
        def _(side=side):
            slab_ref[:, side] = jnp.zeros((POWERS, NV, NRHS, LR, NT), jnp.float32)

        @pl.when(jnp.logical_not(present[3 - side]))
        def _(side=side):
            edge_ref[:, side] = jnp.zeros((POWERS, NV, NRHS, LS, NT), jnp.float32)

    greeted = n_first - 1 + n_second - 1
    for j in range(4):
        greeted = greeted + present[j].astype(jnp.int32)
    pl.semaphore_wait(barrier, greeted)

    def halo_copy(k, j):
        if j < 2:
            start = ROWS - LR if j == 0 else 0
            whole = right_hbm if k == 0 else y_ref.at[k]
            src = whole.at[:, :, pl.ds(start, LR), :]
            dst = slab_ref.at[k, j]
        else:
            src = pack_ref.at[k, 3 - j]
            dst = edge_ref.at[k, j - 2]
        return pltpu.make_async_remote_copy(
            src_ref=src,
            dst_ref=dst,
            send_sem=halo_send.at[k, j],
            recv_sem=halo_recv.at[k, j],
            device_id=peers[j],
            device_id_type=MESH,
        )

    def send_halo(k, js):
        for j in js:

            @pl.when(present[j])
            def _(j=j):
                halo_copy(k, j).start()

    def wait_halo(k):
        for j in range(4):

            @pl.when(present[source_of[j]])
            def _(j=j):
                halo_copy(k, j).wait_recv()

    send_halo(0, (0, 1))
    loads[0].wait()
    for side in range(2):
        rows = pl.ds(0 if side == 0 else LR - 1, LS, stride=LR)
        for a in range(NV):
            for r in range(NRHS):
                pack_ref[0, side, a, r] = y_ref[0, a, r, rows, :]
    send_halo(0, (2, 3))
    loads[1].wait()
    loads[2].wait()

    stores = []
    for k in range(POWERS):
        scale = RAISE if k == 0 else 1.0
        target = y_ref.at[k + 1]
        apply_inner(y_ref.at[k], target, diag_ref, face_ref, w_ref, x_ref, q_ref, scale)
        wait_halo(k)
        last = k == POWERS - 1
        add_halo(
            target,
            face_ref,
            w_ref,
            x_ref,
            (slab_ref[k, 0], slab_ref[k, 1]),
            (edge_ref[k, 0], edge_ref[k, 1]),
            None if last else pack_ref.at[k + 1],
            scale,
        )
        if not last:
            send_halo(k + 1, range(4))
        store = pltpu.make_async_copy(
            target.at[:, :, pl.ds(0, ROWS), :], y_hbm.at[k], out_sem.at[k]
        )
        store.start()
        stores.append(store)

    def reduce_over(value, slots, send, recv, count, me, peer):
        slots[me] = value
        copies = []
        for offset in range(1, count):
            copies.append(
                pltpu.make_async_remote_copy(
                    src_ref=slots.at[me],
                    dst_ref=slots.at[me],
                    send_sem=send.at[offset],
                    recv_sem=recv.at[offset],
                    device_id=peer(offset),
                    device_id_type=MESH,
                )
            )
        for copy in copies:
            copy.start()
        for copy in copies:
            copy.wait()
        total = slots[0]
        for index in range(1, count):
            total = total + slots[index]
        return total

    gram = local_gram(y_ref, m_ref)
    gram = reduce_over(gram, first_ref, first_send, first_recv, n_first, me_first, first_peer)
    gram = reduce_over(gram, second_ref, second_send, second_recv, n_second, chip, second_peer)
    gram_ref[...] = gram
    for k in range(POWERS):
        for j in range(4):

            @pl.when(present[j])
            def _(k=k, j=j):
                halo_copy(k, j).wait_send()

    for store in stores:
        store.wait()


def krylov(n_stream, n_radial, right, diag, face, jac):
    any_spec = pl.BlockSpec(memory_space=pl.ANY)
    f32 = jnp.float32
    dma = pltpu.SemaphoreType.DMA
    n_first = 2 * n_radial
    n_second = n_stream // 2
    return pl.pallas_call(
        functools.partial(krylov_kernel, n_stream, n_radial),
        out_shape=(
            jax.ShapeDtypeStruct((POWERS, NV, NRHS, ROWS, NT), f32),
            jax.ShapeDtypeStruct((NCOL, NT), f32),
        ),
        in_specs=[any_spec, any_spec, any_spec, pl.BlockSpec(memory_space=pltpu.SMEM)],
        out_specs=(any_spec, pl.BlockSpec(memory_space=pltpu.VMEM)),
        scratch_shapes=[
            pltpu.VMEM((POWERS + 1, NV, NRHS, ROWS + LR, NT), f32),
            pltpu.VMEM((NV, NV, ROWS, NT), f32),
            pltpu.VMEM((6, ROWS, NT), f32),
            pltpu.VMEM((len(DIRS) * BLK, KDIM), jnp.bfloat16),
            pltpu.VMEM((KDIM, NRHS * NT), jnp.bfloat16),
            pltpu.VMEM((6 * BLK, NRHS * NT), f32),
            pltpu.VMEM((POWERS, 2, NV, NRHS, LR, NT), f32),
            pltpu.VMEM((POWERS, 2, NV, NRHS, LS, NT), f32),
            pltpu.VMEM((POWERS, 2, NV, NRHS, LS, NT), f32),
            pltpu.VMEM((ROWS, ROWS), f32),
            pltpu.VMEM((n_first, NCOL, NT), f32),
            pltpu.VMEM((n_second, NCOL, NT), f32),
            dma((3,)),
            dma((POWERS,)),
            dma((POWERS, 4)),
            dma((POWERS, 4)),
            dma((n_first,)),
            dma((n_first,)),
            dma((n_second,)),
            dma((n_second,)),
        ],
        compiler_params=pltpu.CompilerParams(collective_id=0, has_side_effects=True),
    )(right, diag, face, jac)


def factor(gram_ref, r_ref, c_ref):
    row = lax.broadcasted_iota(jnp.int32, (NCOL, NT), 0)
    col = lax.broadcasted_iota(jnp.int32, (NCOL, NT), 1)
    twice = gram_ref[...]
    gram = 0.5 * (twice[:, :NCOL] + twice[:, :NCOL].T)
    gram = jnp.concatenate([gram, jnp.zeros((NCOL, NT - NCOL), jnp.float32)], axis=1)
    on_diag = jnp.where(row == col, gram, 0.0)
    down = 1.0 / jnp.sqrt(jnp.sum(on_diag, axis=1, keepdims=True))
    across = jnp.sum(on_diag, axis=0, keepdims=True)
    across = 1.0 / jnp.sqrt(jnp.where(col[:1] < NCOL, across, 1.0))
    work = gram * down * across
    work = jnp.where(col == row + NCOL, 1.0, work)
    for i in range(NCOL):
        lead = work[:, i : i + 1]
        root = 1.0 / jnp.sqrt(work[i : i + 1, i : i + 1])
        line = work[i : i + 1, :] * root
        work = jnp.where(row == i, line, jnp.where(row > i, work - (lead * root) * line, work))
    r_ref[...] = jnp.where(row <= col, work, 0.0)[:, :NCOL]
    for i in range(NCOL):
        lifted = work[:, NCOL + i : NCOL + i + 1] * across[:, i : i + 1]
        c_ref[i] = jnp.broadcast_to(lifted, (NCOL, NT))


def basis_kernel(slabs, gram_ref, right_ref, y_ref, q_ref, r_ref, c_ref):
    @pl.when(pl.program_id(0) == 0)
    def _():
        factor(gram_ref, r_ref, c_ref)

    def step(t, carry):
        a = t // slabs
        here = pl.ds(pl.multiple_of((t % slabs) * LR, LR), LR)
        values = [right_ref[a, r, here, :] for r in range(NRHS)]
        for k in range(POWERS):
            values += [y_ref[k, a, r, here, :] for r in range(NRHS)]
        for j in range(NCOL):
            total = c_ref[0, j : j + 1, :] * values[0]
            for i in range(1, j + 1):
                total = total + c_ref[i, j : j + 1, :] * values[i]
            q_ref[a, j, here, :] = total
        return carry

    lax.fori_loop(0, NV * slabs, step, 0)


def basis(gram, right, ys):
    slabs = 2
    rows = slabs * LR
    f32 = jnp.float32
    return pl.pallas_call(
        functools.partial(basis_kernel, slabs),
        grid=(LS // slabs,),
        out_shape=(
            jax.ShapeDtypeStruct((NV, NCOL, ROWS, NT), f32),
            jax.ShapeDtypeStruct((NCOL, NCOL), f32),
        ),
        in_specs=[
            pl.BlockSpec((NCOL, NT), lambda s: (0, 0)),
            pl.BlockSpec((NV, NRHS, rows, NT), lambda s: (0, 0, s, 0)),
            pl.BlockSpec((POWERS, NV, NRHS, rows, NT), lambda s: (0, 0, 0, s, 0)),
        ],
        out_specs=(
            pl.BlockSpec((NV, NCOL, rows, NT), lambda s: (0, 0, s, 0)),
            pl.BlockSpec((NCOL, NCOL), lambda s: (0, 0)),
        ),
        scratch_shapes=[pltpu.VMEM((NCOL, NCOL, NT), f32)],
    )(gram, right, ys)


def body(n_stream, n_radial, right_side, diag_block, face_coef, jacobians):
    right = right_side.reshape(NV, NRHS, ROWS, NT)
    diag = diag_block.reshape(NV, NV, ROWS, NT)
    face = face_coef.reshape(6, ROWS, NT)
    ys, gram = krylov(n_stream, n_radial, right, diag, face, jacobians)
    q, r_factor = basis(gram, right, ys)
    return q.reshape(NV, NCOL, LS, LR, NT), r_factor


def solution(mesh):
    return jax.shard_map(
        functools.partial(body, mesh.shape["stream"], mesh.shape["radial"]),
        mesh=mesh,
        in_specs=(
            P(None, None, "stream", "radial", None),
            P(None, None, "stream", "radial", None),
            P(None, "stream", "radial", None),
            P(),
        ),
        out_specs=(P(None, None, "stream", "radial", None), P()),
        check_vma=False,
    )
```

```python
import functools

import jax
import jax.numpy as jnp
from jax import lax
from jax.experimental import pallas as pl
from jax.experimental.pallas import tpu as pltpu
from jax.sharding import PartitionSpec as P

NV = 5
NRHS = 4
POWERS = 3
NCOL = 16
LS = 16
LR = 16
NT = 128
ROWS = LS * LR
SHIFT = 6.0
BLK = NV * LR
KDIM = 256
OFFSETS = (0, 0, -1, 1, 0, 0)
UNROLL = 4
GRAM_UNROLL = 2
RAISE = 2.0**24
MESH = pl.DeviceIdType.MESH
HIGH = lax.Precision.HIGHEST


def build_operator(jac_ref, w_ref, halo_w_ref):
    col = lax.broadcasted_iota(jnp.int32, (LR, KDIM), 1)
    row = lax.broadcasted_iota(jnp.int32, (LR, KDIM), 0)
    part = col // BLK
    var = (col % BLK) // LR
    cell = col % LR
    masks = {}
    for offset in (-1, 0, 1):
        hit = (cell == row + offset) & (part < 3)
        masks[offset] = [
            jnp.where(hit & (var == b), -1.0, 0.0).astype(jnp.float32) for b in range(NV)
        ]

    def tile(direction, a, offset):
        total = jac_ref[direction, a, 0] * masks[offset][0]
        for b in range(1, NV):
            total = total + jac_ref[direction, a, b] * masks[offset][b]
        head = total.astype(jnp.bfloat16).astype(jnp.float32)
        return jnp.where(part == 1, total - head, head).astype(jnp.bfloat16)

    for a in range(NV):
        for direction, offset in enumerate(OFFSETS):
            start = (a * 6 + direction) * LR
            w_ref[start : start + LR, :] = tile(direction, a, offset)
        for direction in range(4):
            start = direction * BLK + a * LR
            halo_w_ref[start : start + LR, :] = tile(direction, a, 0)


def split_fields(values):
    head = values.astype(jnp.bfloat16)
    tail = (values - head.astype(jnp.float32)).astype(jnp.bfloat16)
    empty = jnp.zeros((KDIM - 3 * BLK, NT), jnp.bfloat16)
    columns = []
    for r in range(NRHS):
        head_r = head[:, r].reshape(BLK, NT)
        tail_r = tail[:, r].reshape(BLK, NT)
        columns.append(jnp.concatenate([head_r, head_r, tail_r, empty], axis=0))
    return jnp.concatenate(columns, axis=1)


def slab(s):
    return pl.ds(pl.multiple_of(s * LR, LR), LR)


def apply_blocks(source, diag_ref, stage, s, scale):
    for half in range(2):
        rows = pl.ds(pl.multiple_of(s * LR + half * 8, 8), 8)
        fields = [[source[b, r, rows, :] for r in range(NRHS)] for b in range(NV)]
        for a in range(NV):
            totals = [None] * NRHS
            for b in range(NV):
                block = diag_ref[a, b, rows, :]
                if scale != 1.0:
                    block = block * scale
                for r in range(NRHS):
                    term = block * fields[b][r]
                    totals[r] = term if b == 0 else totals[r] + term
            for r in range(NRHS):
                stage[a, r, half * 8 : half * 8 + 8, :] = totals[r]


def apply_inner(source, target, diag_ref, face_ref, w_ref, stages, ahead_ref, open_ref, scale):
    cells = [(a, r) for a in range(NV) for r in range(NRHS)]
    ahead_ref[...] = jnp.zeros((NV, NRHS, LR, NT), jnp.float32)
    open_ref[...] = jnp.zeros((NV, NRHS, LR, NT), jnp.float32)

    def step(t, carry):
        s0 = t * UNROLL
        for u in range(UNROLL):
            apply_blocks(source, diag_ref, stages[u], s0 + u, scale)
        ahead = {cell: ahead_ref[cell[0], cell[1]] for cell in cells}
        unfinished = {cell: open_ref[cell[0], cell[1]] for cell in cells}
        for u in range(UNROLL):
            s = s0 + u
            before = jnp.where(s == 0, LS, s - 1) if u == 0 else s - 1
            product = jnp.dot(
                w_ref[...],
                split_fields(source[:, :, slab(s), :]),
                preferred_element_type=jnp.float32,
            )
            face = [face_ref[0, slab(jnp.minimum(s + 1, LS - 1)), :]]
            face.append(face_ref[1, slab(jnp.maximum(s - 1, 0)), :])
            face += [face_ref[d, slab(s), :] for d in range(2, 6)]
            if scale != 1.0:
                face = [weight * scale for weight in face]
            for a, r in cells:

                def part(d, a=a, r=r):
                    start = (a * 6 + d) * LR
                    return product[start : start + LR, r * NT : (r + 1) * NT]

                target[a, r, slab(before), :] = unfinished[a, r] + face[1] * part(1)
                total = face[2] * part(2) + face[3] * part(3)
                total = total + face[4] * pltpu.roll(part(4), 1, 1)
                total = total + face[5] * pltpu.roll(part(5), NT - 1, 1)
                unfinished[a, r] = total + (stages[u][a, r] + ahead[a, r])
                ahead[a, r] = face[0] * part(0)
        for a, r in cells:
            ahead_ref[a, r] = ahead[a, r]
            open_ref[a, r] = unfinished[a, r]
        return carry

    lax.fori_loop(0, LS // UNROLL, step, 0)
    target[:, :, ROWS - LR : ROWS, :] = open_ref[...]


def add_halo(target, face_ref, halo_w_ref, slabs, edges, rows_ref, scale):
    for side in range(2):
        start = 0 if side == 0 else ROWS - LR
        product = jnp.dot(
            halo_w_ref[side * BLK : (side + 1) * BLK, :],
            split_fields(slabs[side]),
            preferred_element_type=jnp.float32,
        )
        weight = face_ref[side, start : start + LR, :] * scale
        for a in range(NV):
            for r in range(NRHS):
                target[a, r, start : start + LR, :] = target[a, r, start : start + LR, :] + (
                    weight * product[a * LR : (a + 1) * LR, r * NT : (r + 1) * NT]
                )
    for side in range(2):
        rows = pl.ds(0 if side == 0 else LR - 1, LS, stride=LR)
        product = jnp.dot(
            halo_w_ref[(2 + side) * BLK : (3 + side) * BLK, :],
            split_fields(edges[side]),
            preferred_element_type=jnp.float32,
        )
        weight = face_ref[2 + side, rows, :] * scale
        for a in range(NV):
            for r in range(NRHS):
                fresh = target[a, r, rows, :] + weight * (
                    product[a * LR : (a + 1) * LR, r * NT : (r + 1) * NT]
                )
                target[a, r, rows, :] = fresh
                if rows_ref is not None:
                    rows_ref[side, a, r] = fresh


def local_gram(ys, m_ref):
    m_ref[...] = jnp.zeros((ROWS, ROWS), jnp.float32)

    def step(t, carry):
        left = []
        right = []
        for u in range(GRAM_UNROLL * NV):
            s = t * GRAM_UNROLL + u // NV
            a = u % NV
            here = pl.ds(pl.multiple_of(s * LR, LR), LR)
            values = jnp.concatenate(
                [y_ref[a, :, here, :].reshape(NRHS * LR, NT) for y_ref in ys], axis=0
            )
            head = values.astype(jnp.bfloat16)
            tail = (2.0 * (values - head.astype(jnp.float32))).astype(jnp.bfloat16)
            left += [head, tail]
            right += [head, head]
        m_ref[...] += lax.dot_general(
            jnp.concatenate(left, axis=1),
            jnp.concatenate(right, axis=1),
            (((1,), (1,)), ((), ())),
            preferred_element_type=jnp.float32,
        )
        return carry

    lax.fori_loop(0, LS // GRAM_UNROLL, step, 0)
    row = lax.broadcasted_iota(jnp.int32, (ROWS, ROWS), 0)
    col = lax.broadcasted_iota(jnp.int32, (ROWS, ROWS), 1)
    kept = jnp.where(row % LR == col % LR, m_ref[...], 0.0)
    pick_row = lax.broadcasted_iota(jnp.int32, (NCOL, ROWS), 0)
    pick_col = lax.broadcasted_iota(jnp.int32, (NCOL, ROWS), 1)
    pick = jnp.where(pick_col // LR == pick_row, 1.0, 0.0).astype(jnp.float32)
    wide_row = lax.broadcasted_iota(jnp.int32, (NT, ROWS), 0)
    wide_col = lax.broadcasted_iota(jnp.int32, (NT, ROWS), 1)
    wide = jnp.where(wide_col // LR == wide_row, 1.0, 0.0).astype(jnp.float32)
    half = jnp.dot(pick, kept, precision=HIGH, preferred_element_type=jnp.float32)
    return lax.dot_general(
        half, wide, (((1,), (1,)), ((), ())), precision=HIGH, preferred_element_type=jnp.float32
    )


def krylov_kernel(
    n_stream,
    n_radial,
    right_hbm,
    diag_hbm,
    face_hbm,
    jac_hbm,
    y_hbm,
    gram_ref,
    y0_ref,
    y1_ref,
    y2_ref,
    y3_ref,
    diag_ref,
    face_ref,
    jac_ref,
    w_ref,
    halo_w_ref,
    stage0_ref,
    stage1_ref,
    stage2_ref,
    stage3_ref,
    ahead_ref,
    open_ref,
    slab_ref,
    edge_ref,
    pack_ref,
    m_ref,
    first_ref,
    second_ref,
    load_sem,
    out_sem,
    halo_send,
    halo_recv,
    first_send,
    first_recv,
    second_send,
    second_recv,
):
    ys = (y0_ref, y1_ref, y2_ref, y3_ref)
    stages = (stage0_ref, stage1_ref, stage2_ref, stage3_ref)
    si = lax.axis_index("stream")
    ri = lax.axis_index("radial")
    core = si % 2
    chip = si // 2
    n_first = 2 * n_radial
    n_second = n_stream // 2
    me_first = ri * 2 + core

    def first_peer(offset):
        other = (me_first + offset) % n_first
        return (chip * 2 + other % 2, other // 2)

    def second_peer(offset):
        return (((chip + offset) % n_second) * 2 + core, ri)

    loads = [
        pltpu.make_async_copy(right_hbm, y0_ref.at[:, :, pl.ds(0, ROWS), :], load_sem.at[0]),
        pltpu.make_async_copy(face_hbm, face_ref, load_sem.at[1]),
        pltpu.make_async_copy(diag_hbm, diag_ref, load_sem.at[2]),
        pltpu.make_async_copy(jac_hbm, jac_ref, load_sem.at[3]),
    ]
    for load in loads:
        load.start()

    barrier = pltpu.get_barrier_semaphore()
    for offset in range(1, n_first):
        pl.semaphore_signal(barrier, inc=1, device_id=first_peer(offset), device_id_type=MESH)
    for offset in range(1, n_second):
        pl.semaphore_signal(barrier, inc=1, device_id=second_peer(offset), device_id_type=MESH)
    peers = ((si + 1, ri), (si - 1, ri), (si, ri + 1), (si, ri - 1))
    present = (si < n_stream - 1, si > 0, ri < n_radial - 1, ri > 0)
    source_of = (1, 0, 3, 2)
    for j in range(4):

        @pl.when(present[j])
        def _(j=j):
            pl.semaphore_signal(barrier, inc=1, device_id=peers[j], device_id_type=MESH)

    loads[3].wait()
    build_operator(jac_ref, w_ref, halo_w_ref)
    for side in range(2):

        @pl.when(jnp.logical_not(present[1 - side]))
        def _(side=side):
            slab_ref[:, side] = jnp.zeros((POWERS, NV, NRHS, LR, NT), jnp.float32)

        @pl.when(jnp.logical_not(present[3 - side]))
        def _(side=side):
            edge_ref[:, side] = jnp.zeros((POWERS, NV, NRHS, LS, NT), jnp.float32)

    greeted = n_first - 1 + n_second - 1
    for j in range(4):
        greeted = greeted + present[j].astype(jnp.int32)
    pl.semaphore_wait(barrier, greeted)

    def halo_copy(k, j):
        if j < 2:
            start = ROWS - LR if j == 0 else 0
            whole = right_hbm if k == 0 else ys[k]
            src = whole.at[:, :, pl.ds(start, LR), :]
            dst = slab_ref.at[k, j]
        else:
            src = pack_ref.at[k, 3 - j]
            dst = edge_ref.at[k, j - 2]
        return pltpu.make_async_remote_copy(
            src_ref=src,
            dst_ref=dst,
            send_sem=halo_send.at[k, j],
            recv_sem=halo_recv.at[k, j],
            device_id=peers[j],
            device_id_type=MESH,
        )

    def send_halo(k, js):
        for j in js:

            @pl.when(present[j])
            def _(j=j):
                halo_copy(k, j).start()

    def wait_halo(k):
        for j in range(4):

            @pl.when(present[source_of[j]])
            def _(j=j):
                halo_copy(k, j).wait_recv()

    send_halo(0, (0, 1))
    loads[0].wait()
    for side in range(2):
        rows = pl.ds(0 if side == 0 else LR - 1, LS, stride=LR)
        for a in range(NV):
            for r in range(NRHS):
                pack_ref[0, side, a, r] = y0_ref[a, r, rows, :]
    send_halo(0, (2, 3))
    loads[1].wait()
    loads[2].wait()
    for a in range(NV):
        diag_ref[a, a] = diag_ref[a, a] - SHIFT

    stores = []
    for k in range(POWERS):
        scale = RAISE if k == 0 else 1.0
        target = ys[k + 1]
        apply_inner(
            ys[k], target, diag_ref, face_ref, w_ref, stages, ahead_ref, open_ref, scale
        )
        wait_halo(k)
        last = k == POWERS - 1
        add_halo(
            target,
            face_ref,
            halo_w_ref,
            (slab_ref[k, 0], slab_ref[k, 1]),
            (edge_ref[k, 0], edge_ref[k, 1]),
            None if last else pack_ref.at[k + 1],
            scale,
        )
        if not last:
            send_halo(k + 1, range(4))
        store = pltpu.make_async_copy(
            target.at[:, :, pl.ds(0, ROWS), :], y_hbm.at[k], out_sem.at[k]
        )
        store.start()
        stores.append(store)

    def reduce_over(value, slots, send, recv, count, me, peer):
        slots[me] = value
        copies = []
        for offset in range(1, count):
            copies.append(
                pltpu.make_async_remote_copy(
                    src_ref=slots.at[me],
                    dst_ref=slots.at[me],
                    send_sem=send.at[offset],
                    recv_sem=recv.at[offset],
                    device_id=peer(offset),
                    device_id_type=MESH,
                )
            )
        for copy in copies:
            copy.start()
        for copy in copies:
            copy.wait()
        total = slots[0]
        for index in range(1, count):
            total = total + slots[index]
        return total

    gram = local_gram(ys, m_ref)
    gram = reduce_over(gram, first_ref, first_send, first_recv, n_first, me_first, first_peer)
    gram = reduce_over(gram, second_ref, second_send, second_recv, n_second, chip, second_peer)
    gram_ref[...] = gram
    for k in range(POWERS):
        for j in range(4):

            @pl.when(present[j])
            def _(k=k, j=j):
                halo_copy(k, j).wait_send()

    for store in stores:
        store.wait()


def krylov(n_stream, n_radial, right, diag, face, jac):
    any_spec = pl.BlockSpec(memory_space=pl.ANY)
    f32 = jnp.float32
    dma = pltpu.SemaphoreType.DMA
    n_first = 2 * n_radial
    n_second = n_stream // 2
    return pl.pallas_call(
        functools.partial(krylov_kernel, n_stream, n_radial),
        out_shape=(
            jax.ShapeDtypeStruct((POWERS, NV, NRHS, ROWS, NT), f32),
            jax.ShapeDtypeStruct((NCOL, NT), f32),
        ),
        in_specs=[any_spec, any_spec, any_spec, any_spec],
        out_specs=(any_spec, pl.BlockSpec(memory_space=pltpu.VMEM)),
        scratch_shapes=[
            pltpu.VMEM((NV, NRHS, ROWS + LR, NT), f32),
            pltpu.VMEM((NV, NRHS, ROWS + LR, NT), f32),
            pltpu.VMEM((NV, NRHS, ROWS + LR, NT), f32),
            pltpu.VMEM((NV, NRHS, ROWS + LR, NT), f32),
            pltpu.VMEM((NV, NV, ROWS, NT), f32),
            pltpu.VMEM((6, ROWS, NT), f32),
            pltpu.SMEM((6, NV, NV), f32),
            pltpu.VMEM((6 * BLK, KDIM), jnp.bfloat16),
            pltpu.VMEM((4 * BLK, KDIM), jnp.bfloat16),
            pltpu.VMEM((NV, NRHS, LR, NT), f32),
            pltpu.VMEM((NV, NRHS, LR, NT), f32),
            pltpu.VMEM((NV, NRHS, LR, NT), f32),
            pltpu.VMEM((NV, NRHS, LR, NT), f32),
            pltpu.VMEM((NV, NRHS, LR, NT), f32),
            pltpu.VMEM((NV, NRHS, LR, NT), f32),
            pltpu.VMEM((POWERS, 2, NV, NRHS, LR, NT), f32),
            pltpu.VMEM((POWERS, 2, NV, NRHS, LS, NT), f32),
            pltpu.VMEM((POWERS, 2, NV, NRHS, LS, NT), f32),
            pltpu.VMEM((ROWS, ROWS), f32),
            pltpu.VMEM((n_first, NCOL, NT), f32),
            pltpu.VMEM((n_second, NCOL, NT), f32),
            dma((4,)),
            dma((POWERS,)),
            dma((POWERS, 4)),
            dma((POWERS, 4)),
            dma((n_first,)),
            dma((n_first,)),
            dma((n_second,)),
            dma((n_second,)),
        ],
        compiler_params=pltpu.CompilerParams(collective_id=0, has_side_effects=True),
    )(right, diag, face, jac)


def factor(gram_ref, r_ref, c_ref):
    row = lax.broadcasted_iota(jnp.int32, (NCOL, NT), 0)
    col = lax.broadcasted_iota(jnp.int32, (NCOL, NT), 1)
    twice = gram_ref[...]
    gram = 0.5 * (twice[:, :NCOL] + twice[:, :NCOL].T)
    gram = jnp.concatenate([gram, jnp.zeros((NCOL, NT - NCOL), jnp.float32)], axis=1)
    on_diag = jnp.where(row == col, gram, 0.0)
    down = 1.0 / jnp.sqrt(jnp.sum(on_diag, axis=1, keepdims=True))
    across = jnp.sum(on_diag, axis=0, keepdims=True)
    across = 1.0 / jnp.sqrt(jnp.where(col[:1] < NCOL, across, 1.0))
    work = gram * down * across
    work = jnp.where(col == row + NCOL, 1.0, work)
    for i in range(NCOL):
        lead = work[:, i : i + 1]
        root = 1.0 / jnp.sqrt(work[i : i + 1, i : i + 1])
        line = work[i : i + 1, :] * root
        work = jnp.where(row == i, line, jnp.where(row > i, work - (lead * root) * line, work))
    r_ref[...] = jnp.where(row <= col, work, 0.0)[:, :NCOL]
    for i in range(NCOL):
        lifted = work[:, NCOL + i : NCOL + i + 1] * across[:, i : i + 1]
        c_ref[i] = jnp.broadcast_to(lifted, (NCOL, NT))


def basis_kernel(slabs, gram_ref, right_ref, y_ref, q_ref, r_ref, c_ref):
    @pl.when(pl.program_id(0) == 0)
    def _():
        factor(gram_ref, r_ref, c_ref)

    def step(t, carry):
        a = t // slabs
        here = pl.ds(pl.multiple_of((t % slabs) * LR, LR), LR)
        values = [right_ref[a, r, here, :] for r in range(NRHS)]
        for k in range(POWERS):
            values += [y_ref[k, a, r, here, :] for r in range(NRHS)]
        for j in range(NCOL):
            total = c_ref[0, j : j + 1, :] * values[0]
            for i in range(1, j + 1):
                total = total + c_ref[i, j : j + 1, :] * values[i]
            q_ref[a, j, here, :] = total
        return carry

    lax.fori_loop(0, NV * slabs, step, 0)


def basis(gram, right, ys):
    slabs = 2
    rows = slabs * LR
    f32 = jnp.float32
    return pl.pallas_call(
        functools.partial(basis_kernel, slabs),
        grid=(LS // slabs,),
        out_shape=(
            jax.ShapeDtypeStruct((NV, NCOL, ROWS, NT), f32),
            jax.ShapeDtypeStruct((NCOL, NCOL), f32),
        ),
        in_specs=[
            pl.BlockSpec((NCOL, NT), lambda s: (0, 0)),
            pl.BlockSpec((NV, NRHS, rows, NT), lambda s: (0, 0, s, 0)),
            pl.BlockSpec((POWERS, NV, NRHS, rows, NT), lambda s: (0, 0, 0, s, 0)),
        ],
        out_specs=(
            pl.BlockSpec((NV, NCOL, rows, NT), lambda s: (0, 0, s, 0)),
            pl.BlockSpec((NCOL, NCOL), lambda s: (0, 0)),
        ),
        scratch_shapes=[pltpu.VMEM((NCOL, NCOL, NT), f32)],
    )(gram, right, ys)


def body(n_stream, n_radial, right_side, diag_block, face_coef, jacobians):
    right = right_side.reshape(NV, NRHS, ROWS, NT)
    diag = diag_block.reshape(NV, NV, ROWS, NT)
    face = face_coef.reshape(6, ROWS, NT)
    ys, gram = krylov(n_stream, n_radial, right, diag, face, jacobians)
    q, r_factor = basis(gram, right, ys)
    return q.reshape(NV, NCOL, LS, LR, NT), r_factor


def solution(mesh):
    return jax.shard_map(
        functools.partial(body, mesh.shape["stream"], mesh.shape["radial"]),
        mesh=mesh,
        in_specs=(
            P(None, None, "stream", "radial", None),
            P(None, None, "stream", "radial", None),
            P(None, "stream", "radial", None),
            P(),
        ),
        out_specs=(P(None, None, "stream", "radial", None), P()),
        check_vma=False,
    )
```

```python
import functools

import jax
import jax.numpy as jnp
from jax import lax
from jax.experimental import pallas as pl
from jax.experimental.pallas import tpu as pltpu
from jax.sharding import PartitionSpec as P

NV = 5
NRHS = 4
POWERS = 3
NCOL = 16
LS = 16
LR = 16
NT = 128
ROWS = LS * LR
SHIFT = 6.0
BLK = NV * LR
KDIM = 256
OFFSETS = (0, 0, -1, 1, 0, 0)
UNROLL = 4
GRAM_UNROLL = 2
BASIS_SLABS = 2
HALF = 8
RAISE = 2.0**24
MESH = pl.DeviceIdType.MESH
HIGH = lax.Precision.HIGHEST


def build_operator(jac_ref, w_ref, halo_w_ref):
    col = lax.broadcasted_iota(jnp.int32, (LR, KDIM), 1)
    row = lax.broadcasted_iota(jnp.int32, (LR, KDIM), 0)
    part = col // BLK
    var = (col % BLK) // LR
    cell = col % LR
    masks = {}
    for offset in (-1, 0, 1):
        hit = (cell == row + offset) & (part < 3)
        masks[offset] = [
            jnp.where(hit & (var == b), -1.0, 0.0).astype(jnp.float32) for b in range(NV)
        ]

    def tile(direction, a, offset):
        total = jac_ref[a, direction, 0] * masks[offset][0]
        for b in range(1, NV):
            total = total + jac_ref[a, direction, b] * masks[offset][b]
        head = total.astype(jnp.bfloat16).astype(jnp.float32)
        return jnp.where(part == 1, total - head, head).astype(jnp.bfloat16)

    for a in range(NV):
        for direction, offset in enumerate(OFFSETS):
            start = (a * 6 + direction) * LR
            w_ref[start : start + LR, :] = tile(direction, a, offset)
        for direction in range(4):
            start = direction * BLK + a * LR
            halo_w_ref[start : start + LR, :] = tile(direction, a, 0)


def split_fields(values):
    head = values.astype(jnp.bfloat16)
    tail = (values - head.astype(jnp.float32)).astype(jnp.bfloat16)
    empty = jnp.zeros((KDIM - 3 * BLK, NT), jnp.bfloat16)
    columns = []
    for r in range(NRHS):
        head_r = head[:, r].reshape(BLK, NT)
        tail_r = tail[:, r].reshape(BLK, NT)
        columns.append(jnp.concatenate([head_r, head_r, tail_r, empty], axis=0))
    return jnp.concatenate(columns, axis=1)


def slab(s):
    return pl.ds(pl.multiple_of(s * LR, LR), LR)


def apply_blocks(source, diag_ref, stage, s, scale):
    for half in range(2):
        rows = pl.ds(pl.multiple_of(s * LR + half * 8, 8), 8)
        fields = [[source[b, r, rows, :] for r in range(NRHS)] for b in range(NV)]
        for a in range(NV):
            totals = [None] * NRHS
            for b in range(NV):
                block = diag_ref[a, b, rows, :]
                if scale != 1.0:
                    block = block * scale
                for r in range(NRHS):
                    term = block * fields[b][r]
                    totals[r] = term if b == 0 else totals[r] + term
            for r in range(NRHS):
                stage[a, r, half * 8 : half * 8 + 8, :] = totals[r]


def apply_inner(source, target, diag_ref, face_ref, w_ref, stages, ahead_ref, open_ref, scale):
    cells = [(a, r) for a in range(NV) for r in range(NRHS)]
    ahead_ref[...] = jnp.zeros((NV, NRHS, LR, NT), jnp.float32)
    open_ref[...] = jnp.zeros((NV, NRHS, LR, NT), jnp.float32)

    def step(t, carry):
        s0 = t * UNROLL
        for u in range(UNROLL):
            apply_blocks(source, diag_ref, stages[u], s0 + u, scale)
        ahead = {cell: ahead_ref[cell[0], cell[1]] for cell in cells}
        unfinished = {cell: open_ref[cell[0], cell[1]] for cell in cells}
        for u in range(UNROLL):
            s = s0 + u
            before = jnp.where(s == 0, LS, s - 1) if u == 0 else s - 1
            product = jnp.dot(
                w_ref[...],
                split_fields(source[:, :, slab(s), :]),
                preferred_element_type=jnp.float32,
            )
            face = [face_ref[0, slab(jnp.minimum(s + 1, LS - 1)), :]]
            face.append(face_ref[1, slab(jnp.maximum(s - 1, 0)), :])
            face += [face_ref[d, slab(s), :] for d in range(2, 6)]
            if scale != 1.0:
                face = [weight * scale for weight in face]
            for a, r in cells:

                def part(d, a=a, r=r):
                    start = (a * 6 + d) * LR
                    return product[start : start + LR, r * NT : (r + 1) * NT]

                target[a, r, slab(before), :] = unfinished[a, r] + face[1] * part(1)
                total = face[2] * part(2) + face[3] * part(3)
                total = total + face[4] * pltpu.roll(part(4), 1, 1)
                total = total + face[5] * pltpu.roll(part(5), NT - 1, 1)
                unfinished[a, r] = total + (stages[u][a, r] + ahead[a, r])
                ahead[a, r] = face[0] * part(0)
        for a, r in cells:
            ahead_ref[a, r] = ahead[a, r]
            open_ref[a, r] = unfinished[a, r]
        return carry

    lax.fori_loop(0, LS // UNROLL, step, 0)
    target[:, :, ROWS - LR : ROWS, :] = open_ref[...]


def add_halo(target, face_ref, halo_w_ref, slabs, edges, rows_ref, scale):
    for side in range(2):
        start = 0 if side == 0 else ROWS - LR
        product = jnp.dot(
            halo_w_ref[side * BLK : (side + 1) * BLK, :],
            split_fields(slabs[side]),
            preferred_element_type=jnp.float32,
        )
        weight = face_ref[side, start : start + LR, :] * scale
        for a in range(NV):
            for r in range(NRHS):
                target[a, r, start : start + LR, :] = target[a, r, start : start + LR, :] + (
                    weight * product[a * LR : (a + 1) * LR, r * NT : (r + 1) * NT]
                )
    for side in range(2):
        rows = pl.ds(0 if side == 0 else LR - 1, LS, stride=LR)
        product = jnp.dot(
            halo_w_ref[(2 + side) * BLK : (3 + side) * BLK, :],
            split_fields(edges[side]),
            preferred_element_type=jnp.float32,
        )
        weight = face_ref[2 + side, rows, :] * scale
        for a in range(NV):
            for r in range(NRHS):
                fresh = target[a, r, rows, :] + weight * (
                    product[a * LR : (a + 1) * LR, r * NT : (r + 1) * NT]
                )
                target[a, r, rows, :] = fresh
                if rows_ref is not None:
                    rows_ref[side, a, r] = fresh


def local_gram(ys, m_ref):
    m_ref[...] = jnp.zeros((ROWS, ROWS), jnp.float32)

    def step(t, carry):
        left = []
        right = []
        for u in range(GRAM_UNROLL * NV):
            s = t * GRAM_UNROLL + u // NV
            a = u % NV
            here = pl.ds(pl.multiple_of(s * LR, LR), LR)
            values = jnp.concatenate(
                [y_ref[a, :, here, :].reshape(NRHS * LR, NT) for y_ref in ys], axis=0
            )
            head = values.astype(jnp.bfloat16)
            tail = (2.0 * (values - head.astype(jnp.float32))).astype(jnp.bfloat16)
            left += [head, tail]
            right += [head, head]
        m_ref[...] += lax.dot_general(
            jnp.concatenate(left, axis=1),
            jnp.concatenate(right, axis=1),
            (((1,), (1,)), ((), ())),
            preferred_element_type=jnp.float32,
        )
        return carry

    lax.fori_loop(0, LS // GRAM_UNROLL, step, 0)
    row = lax.broadcasted_iota(jnp.int32, (ROWS, ROWS), 0)
    col = lax.broadcasted_iota(jnp.int32, (ROWS, ROWS), 1)
    kept = jnp.where(row % LR == col % LR, m_ref[...], 0.0)
    pick_row = lax.broadcasted_iota(jnp.int32, (NCOL, ROWS), 0)
    pick_col = lax.broadcasted_iota(jnp.int32, (NCOL, ROWS), 1)
    pick = jnp.where(pick_col // LR == pick_row, 1.0, 0.0).astype(jnp.float32)
    wide_row = lax.broadcasted_iota(jnp.int32, (NT, ROWS), 0)
    wide_col = lax.broadcasted_iota(jnp.int32, (NT, ROWS), 1)
    wide = jnp.where(wide_col // LR == wide_row, 1.0, 0.0).astype(jnp.float32)
    half = jnp.dot(pick, kept, precision=HIGH, preferred_element_type=jnp.float32)
    return lax.dot_general(
        half, wide, (((1,), (1,)), ((), ())), precision=HIGH, preferred_element_type=jnp.float32
    )


def krylov_kernel(
    n_stream,
    n_radial,
    right_hbm,
    diag_hbm,
    face_hbm,
    jac_hbm,
    y0_ref,
    y1_ref,
    y2_ref,
    y3_ref,
    gram_ref,
    diag_ref,
    face_ref,
    jac_ref,
    w_ref,
    halo_w_ref,
    stage0_ref,
    stage1_ref,
    stage2_ref,
    stage3_ref,
    ahead_ref,
    open_ref,
    slab_ref,
    edge_ref,
    pack_ref,
    m_ref,
    first_ref,
    second_ref,
    load_sem,
    halo_send,
    halo_recv,
    first_send,
    first_recv,
    second_send,
    second_recv,
):
    ys = (y0_ref, y1_ref, y2_ref, y3_ref)
    stages = (stage0_ref, stage1_ref, stage2_ref, stage3_ref)
    si = lax.axis_index("stream")
    ri = lax.axis_index("radial")
    core = si % 2
    chip = si // 2
    n_first = 2 * n_radial
    n_second = n_stream // 2
    me_first = ri * 2 + core

    def first_peer(offset):
        other = (me_first + offset) % n_first
        return (chip * 2 + other % 2, other // 2)

    def second_peer(offset):
        return (((chip + offset) % n_second) * 2 + core, ri)

    loads = [
        pltpu.make_async_copy(right_hbm, y0_ref.at[:, :, pl.ds(0, ROWS), :], load_sem.at[0]),
        pltpu.make_async_copy(face_hbm, face_ref, load_sem.at[1]),
        pltpu.make_async_copy(diag_hbm, diag_ref, load_sem.at[2]),
        pltpu.make_async_copy(jac_hbm, jac_ref, load_sem.at[3]),
    ]
    for load in loads:
        load.start()

    barrier = pltpu.get_barrier_semaphore()
    for offset in range(1, n_first):
        pl.semaphore_signal(barrier, inc=1, device_id=first_peer(offset), device_id_type=MESH)
    for offset in range(1, n_second):
        pl.semaphore_signal(barrier, inc=1, device_id=second_peer(offset), device_id_type=MESH)
    peers = ((si + 1, ri), (si - 1, ri), (si, ri + 1), (si, ri - 1))
    present = (si < n_stream - 1, si > 0, ri < n_radial - 1, ri > 0)
    source_of = (1, 0, 3, 2)
    for j in range(4):

        @pl.when(present[j])
        def _(j=j):
            pl.semaphore_signal(barrier, inc=1, device_id=peers[j], device_id_type=MESH)

    loads[3].wait()
    build_operator(jac_ref, w_ref, halo_w_ref)
    for side in range(2):

        @pl.when(jnp.logical_not(present[1 - side]))
        def _(side=side):
            slab_ref[:, side] = jnp.zeros((POWERS, NV, NRHS, LR, NT), jnp.float32)

        @pl.when(jnp.logical_not(present[3 - side]))
        def _(side=side):
            edge_ref[:, side] = jnp.zeros((POWERS, NV, NRHS, LS, NT), jnp.float32)

    greeted = n_first - 1 + n_second - 1
    for j in range(4):
        greeted = greeted + present[j].astype(jnp.int32)
    pl.semaphore_wait(barrier, greeted)

    def halo_copy(k, j):
        if j < 2:
            start = ROWS - LR if j == 0 else 0
            whole = right_hbm if k == 0 else ys[k]
            src = whole.at[:, :, pl.ds(start, LR), :]
            dst = slab_ref.at[k, j]
        else:
            src = pack_ref.at[k, 3 - j]
            dst = edge_ref.at[k, j - 2]
        return pltpu.make_async_remote_copy(
            src_ref=src,
            dst_ref=dst,
            send_sem=halo_send.at[k, j],
            recv_sem=halo_recv.at[k, j],
            device_id=peers[j],
            device_id_type=MESH,
        )

    def send_halo(k, js):
        for j in js:

            @pl.when(present[j])
            def _(j=j):
                halo_copy(k, j).start()

    def wait_halo(k):
        for j in range(4):

            @pl.when(present[source_of[j]])
            def _(j=j):
                halo_copy(k, j).wait_recv()

    send_halo(0, (0, 1))
    loads[0].wait()
    for side in range(2):
        rows = pl.ds(0 if side == 0 else LR - 1, LS, stride=LR)
        for a in range(NV):
            for r in range(NRHS):
                pack_ref[0, side, a, r] = y0_ref[a, r, rows, :]
    send_halo(0, (2, 3))
    loads[1].wait()
    loads[2].wait()
    for a in range(NV):
        diag_ref[a, a] = diag_ref[a, a] - SHIFT

    for k in range(POWERS):
        scale = RAISE if k == 0 else 1.0
        target = ys[k + 1]
        apply_inner(
            ys[k], target, diag_ref, face_ref, w_ref, stages, ahead_ref, open_ref, scale
        )
        wait_halo(k)
        last = k == POWERS - 1
        add_halo(
            target,
            face_ref,
            halo_w_ref,
            (slab_ref[k, 0], slab_ref[k, 1]),
            (edge_ref[k, 0], edge_ref[k, 1]),
            None if last else pack_ref.at[k + 1],
            scale,
        )
        if not last:
            send_halo(k + 1, range(4))

    def reduce_over(value, slots, send, recv, count, me, peer):
        slots[me] = value
        copies = []
        for offset in range(1, count):
            copies.append(
                pltpu.make_async_remote_copy(
                    src_ref=slots.at[me],
                    dst_ref=slots.at[me],
                    send_sem=send.at[offset],
                    recv_sem=recv.at[offset],
                    device_id=peer(offset),
                    device_id_type=MESH,
                )
            )
        for copy in copies:
            copy.start()
        for copy in copies:
            copy.wait()
        total = slots[0]
        for index in range(1, count):
            total = total + slots[index]
        return total

    gram = local_gram(ys, m_ref)
    gram = reduce_over(gram, first_ref, first_send, first_recv, n_first, me_first, first_peer)
    gram = reduce_over(gram, second_ref, second_send, second_recv, n_second, chip, second_peer)
    gram_ref[...] = gram
    for k in range(POWERS):
        for j in range(4):

            @pl.when(present[j])
            def _(k=k, j=j):
                halo_copy(k, j).wait_send()


def krylov(n_stream, n_radial, right, diag, face, jac):
    hbm = pl.BlockSpec(memory_space=pltpu.HBM)
    f32 = jnp.float32
    dma = pltpu.SemaphoreType.DMA
    n_first = 2 * n_radial
    n_second = n_stream // 2
    return pl.pallas_call(
        functools.partial(krylov_kernel, n_stream, n_radial),
        out_shape=(
            *[pltpu.VMEM((NV, NRHS, ROWS + LR, NT), f32)] * (POWERS + 1),
            jax.ShapeDtypeStruct((NCOL, NT), f32),
        ),
        in_specs=[hbm] * 4,
        out_specs=tuple([pl.BlockSpec(memory_space=pltpu.VMEM)] * (POWERS + 2)),
        scratch_shapes=[
            pltpu.VMEM((NV, NV, ROWS, NT), f32),
            pltpu.VMEM((6, ROWS, NT), f32),
            pltpu.SMEM((NV, 6, NV), f32),
            pltpu.VMEM((6 * BLK, KDIM), jnp.bfloat16),
            pltpu.VMEM((4 * BLK, KDIM), jnp.bfloat16),
            pltpu.VMEM((NV, NRHS, LR, NT), f32),
            pltpu.VMEM((NV, NRHS, LR, NT), f32),
            pltpu.VMEM((NV, NRHS, LR, NT), f32),
            pltpu.VMEM((NV, NRHS, LR, NT), f32),
            pltpu.VMEM((NV, NRHS, LR, NT), f32),
            pltpu.VMEM((NV, NRHS, LR, NT), f32),
            pltpu.VMEM((POWERS, 2, NV, NRHS, LR, NT), f32),
            pltpu.VMEM((POWERS, 2, NV, NRHS, LS, NT), f32),
            pltpu.VMEM((POWERS, 2, NV, NRHS, LS, NT), f32),
            pltpu.VMEM((ROWS, ROWS), f32),
            pltpu.VMEM((n_first, NCOL, NT), f32),
            pltpu.VMEM((n_second, NCOL, NT), f32),
            dma((4,)),
            dma((POWERS, 4)),
            dma((POWERS, 4)),
            dma((n_first,)),
            dma((n_first,)),
            dma((n_second,)),
            dma((n_second,)),
        ],
        compiler_params=pltpu.CompilerParams(collective_id=0, has_side_effects=True, vmem_limit_bytes=55_500_000),
    )(right, diag, face, jac)


def factor(gram_ref, r_ref, c_ref):
    row = lax.broadcasted_iota(jnp.int32, (NCOL, NT), 0)
    col = lax.broadcasted_iota(jnp.int32, (NCOL, NT), 1)
    twice = gram_ref[...]
    gram = 0.5 * (twice[:, :NCOL] + twice[:, :NCOL].T)
    gram = jnp.concatenate([gram, jnp.zeros((NCOL, NT - NCOL), jnp.float32)], axis=1)
    on_diag = jnp.where(row == col, gram, 0.0)
    down = 1.0 / jnp.sqrt(jnp.sum(on_diag, axis=1, keepdims=True))
    across = jnp.sum(on_diag, axis=0, keepdims=True)
    across = 1.0 / jnp.sqrt(jnp.where(col[:1] < NCOL, across, 1.0))
    work = gram * down * across
    work = jnp.where(col == row + NCOL, 1.0, work)
    for i in range(NCOL):
        lead = work[:, i : i + 1]
        root = 1.0 / jnp.sqrt(work[i : i + 1, i : i + 1])
        line = work[i : i + 1, :] * root
        work = jnp.where(row == i, line, jnp.where(row > i, work - (lead * root) * line, work))
    r_ref[...] = jnp.where(row <= col, work, 0.0)[:, :NCOL]
    wide = NCOL * HALF
    col_of = lax.broadcasted_iota(jnp.int32, (NCOL, wide), 1)
    row_of = lax.broadcasted_iota(jnp.int32, (NCOL, wide), 0)
    spread = jnp.where(col_of // HALF == row_of, down, 0.0)
    repeat_row = lax.broadcasted_iota(jnp.int32, (wide, NCOL), 0)
    repeat_col = lax.broadcasted_iota(jnp.int32, (wide, NCOL), 1)
    repeat = jnp.where(repeat_row // HALF == repeat_col, 1.0, 0.0).astype(jnp.float32)
    lifted = jnp.dot(
        work[:, NCOL : 2 * NCOL], spread, precision=HIGH, preferred_element_type=jnp.float32
    )
    lifted = jnp.dot(repeat, lifted, precision=HIGH, preferred_element_type=jnp.float32)
    full_row = lax.broadcasted_iota(jnp.int32, (wide, wide), 0)
    full_col = lax.broadcasted_iota(jnp.int32, (wide, wide), 1)
    lifted = jnp.where(full_row % HALF == full_col % HALF, lifted, 0.0)
    head = lifted.astype(jnp.bfloat16)
    tail = (lifted - head.astype(jnp.float32)).astype(jnp.bfloat16)
    c_ref[...] = jnp.concatenate([head, head, tail], axis=1)


def basis_kernel(slabs, gram_ref, y0_ref, y1_ref, y2_ref, y3_ref, q_ref, r_ref, c_ref):
    @pl.when(pl.program_id(0) == 0)
    def _():
        factor(gram_ref, r_ref, c_ref)

    first = pl.program_id(0) * slabs

    def step(a, carry):
        for half in range(LR // HALF):
            columns = []
            for s in range(slabs):
                rows = pl.ds(pl.multiple_of((first + s) * LR + half * HALF, HALF), HALF)
                column = []
                for y_ref in (y0_ref, y1_ref, y2_ref, y3_ref):
                    column += [y_ref[a, r, rows, :] for r in range(NRHS)]
                columns.append(jnp.concatenate(column, axis=0))
            values = jnp.concatenate(columns, axis=1)
            head = values.astype(jnp.bfloat16)
            tail = (values - head.astype(jnp.float32)).astype(jnp.bfloat16)
            stacked = jnp.concatenate([head, tail, head], axis=0)
            product = jnp.dot(c_ref[...], stacked, preferred_element_type=jnp.float32)
            for s in range(slabs):
                rows = slice(s * LR + half * HALF, s * LR + (half + 1) * HALF)
                for j in range(NCOL):
                    q_ref[a, j, rows, :] = product[
                        j * HALF : (j + 1) * HALF, s * NT : (s + 1) * NT
                    ]
        return carry

    lax.fori_loop(0, NV, step, 0)


def basis(gram, fields):
    slabs = BASIS_SLABS
    rows = slabs * LR
    f32 = jnp.float32
    vmem = pl.BlockSpec(memory_space=pltpu.VMEM)
    return pl.pallas_call(
        functools.partial(basis_kernel, slabs),
        grid=(LS // slabs,),
        out_shape=(
            jax.ShapeDtypeStruct((NV, NCOL, ROWS, NT), f32),
            jax.ShapeDtypeStruct((NCOL, NCOL), f32),
        ),
        in_specs=[vmem] * (POWERS + 2),
        out_specs=(
            pl.BlockSpec((NV, NCOL, rows, NT), lambda s: (0, 0, s, 0)),
            pl.BlockSpec((NCOL, NCOL), lambda s: (0, 0)),
        ),
        scratch_shapes=[pltpu.VMEM((NCOL * HALF, 3 * NCOL * HALF), jnp.bfloat16)],
        compiler_params=pltpu.CompilerParams(vmem_limit_bytes=30 * 2**20),
    )(gram, *fields)


def body(n_stream, n_radial, right_side, diag_block, face_coef, jacobians):
    right = right_side.reshape(NV, NRHS, ROWS, NT)
    diag = diag_block.reshape(NV, NV, ROWS, NT)
    face = face_coef.reshape(6, ROWS, NT)
    jac = jnp.transpose(jacobians, (1, 0, 2))
    *fields, gram = krylov(n_stream, n_radial, right, diag, face, jac)
    q, r_factor = basis(gram, fields)
    return q.reshape(NV, NCOL, LS, LR, NT), r_factor


def solution(mesh):
    return jax.shard_map(
        functools.partial(body, mesh.shape["stream"], mesh.shape["radial"]),
        mesh=mesh,
        in_specs=(
            P(None, None, "stream", "radial", None),
            P(None, None, "stream", "radial", None),
            P(None, "stream", "radial", None),
            P(),
        ),
        out_specs=(P(None, None, "stream", "radial", None), P()),
        check_vma=False,
    )
```

```python
import functools

import jax
import jax.numpy as jnp
from jax import lax
from jax.experimental import pallas as pl
from jax.experimental.pallas import tpu as pltpu
from jax.sharding import PartitionSpec as P

NV = 5
NRHS = 4
POWERS = 3
NCOL = 16
LS = 16
LR = 16
NT = 128
ROWS = LS * LR
SHIFT = 6.0
BLK = NV * LR
KDIM = 256
OFFSETS = (0, 0, -1, 1, 0, 0)
UNROLL = 4
GRAM_ROWS = 32
GRAM_CHUNKS = ROWS // GRAM_ROWS
DONE = 12
RAISE = 2.0**24
MESH = pl.DeviceIdType.MESH


def build_operator(jac_ref, w_ref, halo_w_ref):
    col = lax.broadcasted_iota(jnp.int32, (LR, KDIM), 1)
    row = lax.broadcasted_iota(jnp.int32, (LR, KDIM), 0)
    part = col // BLK
    var = (col % BLK) // LR
    cell = col % LR
    masks = {}
    for offset in (-1, 0, 1):
        hit = (cell == row + offset) & (part < 3)
        masks[offset] = [
            jnp.where(hit & (var == b), -1.0, 0.0).astype(jnp.float32) for b in range(NV)
        ]

    def tile(direction, a, offset):
        total = jac_ref[a, direction, 0] * masks[offset][0]
        for b in range(1, NV):
            total = total + jac_ref[a, direction, b] * masks[offset][b]
        head = total.astype(jnp.bfloat16).astype(jnp.float32)
        return jnp.where(part == 1, total - head, head).astype(jnp.bfloat16)

    for a in range(NV):
        for direction, offset in enumerate(OFFSETS):
            start = (a * 6 + direction) * LR
            w_ref[start : start + LR, :] = tile(direction, a, offset)
        for direction in range(4):
            start = direction * BLK + a * LR
            halo_w_ref[start : start + LR, :] = tile(direction, a, 0)


def split_fields(values):
    head = values.astype(jnp.bfloat16)
    tail = (values - head.astype(jnp.float32)).astype(jnp.bfloat16)
    empty = jnp.zeros((KDIM - 3 * BLK, NT), jnp.bfloat16)
    columns = []
    for r in range(NRHS):
        head_r = head[:, r].reshape(BLK, NT)
        tail_r = tail[:, r].reshape(BLK, NT)
        columns.append(jnp.concatenate([head_r, head_r, tail_r, empty], axis=0))
    return jnp.concatenate(columns, axis=1)


def slab(s):
    return pl.ds(pl.multiple_of(s * LR, LR), LR)


def apply_blocks(source, diag_ref, stage, s, scale):
    for half in range(2):
        rows = pl.ds(pl.multiple_of(s * LR + half * 8, 8), 8)
        fields = [[source[b, r, rows, :] for r in range(NRHS)] for b in range(NV)]
        for a in range(NV):
            totals = [None] * NRHS
            for b in range(NV):
                block = diag_ref[a, b, rows, :]
                if scale != 1.0:
                    block = block * scale
                for r in range(NRHS):
                    term = block * fields[b][r]
                    totals[r] = term if b == 0 else totals[r] + term
            for r in range(NRHS):
                stage[a, r, half * 8 : half * 8 + 8, :] = totals[r]


def apply_inner(source, target, diag_ref, face_ref, w_ref, stages, ahead_ref, open_ref, scale):
    cells = [(a, r) for a in range(NV) for r in range(NRHS)]
    ahead_ref[...] = jnp.zeros((NV, NRHS, LR, NT), jnp.float32)
    open_ref[...] = jnp.zeros((NV, NRHS, LR, NT), jnp.float32)

    def step(t, carry):
        s0 = t * UNROLL
        for u in range(UNROLL):
            apply_blocks(source, diag_ref, stages[u], s0 + u, scale)
        ahead = {cell: ahead_ref[cell[0], cell[1]] for cell in cells}
        unfinished = {cell: open_ref[cell[0], cell[1]] for cell in cells}
        for u in range(UNROLL):
            s = s0 + u
            before = jnp.where(s == 0, LS, s - 1) if u == 0 else s - 1
            product = jnp.dot(
                w_ref[...],
                split_fields(source[:, :, slab(s), :]),
                preferred_element_type=jnp.float32,
            )
            face = [face_ref[0, slab(jnp.minimum(s + 1, LS - 1)), :]]
            face.append(face_ref[1, slab(jnp.maximum(s - 1, 0)), :])
            face += [face_ref[d, slab(s), :] for d in range(2, 6)]
            if scale != 1.0:
                face = [weight * scale for weight in face]
            for a, r in cells:

                def part(d, a=a, r=r):
                    start = (a * 6 + d) * LR
                    return product[start : start + LR, r * NT : (r + 1) * NT]

                target[a, r, slab(before), :] = unfinished[a, r] + face[1] * part(1)
                total = face[2] * part(2) + face[3] * part(3)
                total = total + face[4] * pltpu.roll(part(4), 1, 1)
                total = total + face[5] * pltpu.roll(part(5), NT - 1, 1)
                unfinished[a, r] = total + (stages[u][a, r] + ahead[a, r])
                ahead[a, r] = face[0] * part(0)
        for a, r in cells:
            ahead_ref[a, r] = ahead[a, r]
            open_ref[a, r] = unfinished[a, r]
        return carry

    lax.fori_loop(0, LS // UNROLL, step, 0)
    target[:, :, ROWS - LR : ROWS, :] = open_ref[...]


def add_halo(target, face_ref, halo_w_ref, slabs, edges, rows_ref, scale):
    for side in range(2):
        start = 0 if side == 0 else ROWS - LR
        product = jnp.dot(
            halo_w_ref[side * BLK : (side + 1) * BLK, :],
            split_fields(slabs[side]),
            preferred_element_type=jnp.float32,
        )
        weight = face_ref[side, start : start + LR, :] * scale
        for a in range(NV):
            for r in range(NRHS):
                target[a, r, start : start + LR, :] = target[a, r, start : start + LR, :] + (
                    weight * product[a * LR : (a + 1) * LR, r * NT : (r + 1) * NT]
                )
    for side in range(2):
        rows = pl.ds(0 if side == 0 else LR - 1, LS, stride=LR)
        product = jnp.dot(
            halo_w_ref[(2 + side) * BLK : (3 + side) * BLK, :],
            split_fields(edges[side]),
            preferred_element_type=jnp.float32,
        )
        weight = face_ref[2 + side, rows, :] * scale
        for a in range(NV):
            for r in range(NRHS):
                fresh = target[a, r, rows, :] + weight * (
                    product[a * LR : (a + 1) * LR, r * NT : (r + 1) * NT]
                )
                target[a, r, rows, :] = fresh
                if rows_ref is not None:
                    rows_ref[side, a, r] = fresh


def gram_block(left, right, acc_ref, k, j):
    pairs = [(p, q) for p in range(NRHS) for q in range(NRHS) if k != j or q <= p]

    def step(t, sums):
        a = t // GRAM_CHUNKS
        rows = pl.ds(pl.multiple_of((t % GRAM_CHUNKS) * GRAM_ROWS, GRAM_ROWS), GRAM_ROWS)
        mine = [left[a, p, rows, :] for p in range(NRHS)]
        other = mine if k == j else [right[a, q, rows, :] for q in range(NRHS)]
        fresh = []
        for index, (p, q) in enumerate(pairs):
            term = mine[p] * other[q]
            total = sums[index]
            for piece in range(GRAM_ROWS // 8):
                total = total + term[piece * 8 : piece * 8 + 8]
            fresh.append(total)
        return tuple(fresh)

    empty = tuple(jnp.zeros((8, NT), jnp.float32) for _ in pairs)
    sums = lax.fori_loop(0, NV * GRAM_CHUNKS, step, empty)
    for index, (p, q) in enumerate(pairs):
        acc_ref[4 * k + p, 4 * j + q] = sums[index]
        if k == j and p != q:
            acc_ref[4 * k + q, 4 * j + p] = sums[index]


def gram_columns(acc_ref, columns):
    lane = lax.broadcasted_iota(jnp.int32, (NCOL, NT), 1)
    table = jnp.zeros((NCOL, NT), jnp.float32)
    for i in columns:
        rows = jnp.sum(acc_ref[i], axis=1)
        table = table + jnp.where(lane == i, jnp.sum(rows, axis=1, keepdims=True), 0.0)
    return table


def eliminate(table, count):
    row = lax.broadcasted_iota(jnp.int32, (NCOL, NT), 0)
    col = lax.broadcasted_iota(jnp.int32, (NCOL, NT), 1)
    square = table[:, :NCOL]
    flipped = jnp.concatenate([square.T, jnp.zeros((NCOL, NT - NCOL), jnp.float32)], axis=1)
    gram = jnp.where((row // NRHS > col // NRHS) & (col < NCOL), flipped, table)
    on_diag = jnp.where(row == col, gram, 0.0)
    down = jnp.sum(on_diag, axis=1, keepdims=True)
    across = jnp.sum(on_diag, axis=0, keepdims=True)
    down = 1.0 / jnp.sqrt(jnp.where(row[:, :1] < count, down, 1.0))
    across = 1.0 / jnp.sqrt(jnp.where(col[:1] < count, across, 1.0))
    work = gram * down * across
    work = jnp.where(col == row + NCOL, 1.0, work)
    for i in range(count):
        lead = work[:, i : i + 1]
        root = 1.0 / jnp.sqrt(work[i : i + 1, i : i + 1])
        line = work[i : i + 1, :] * root
        work = jnp.where(row == i, line, jnp.where(row > i, work - (lead * root) * line, work))
    return work, across


def combine(work, across, fields, c_ref, out_ref, columns):
    last = columns[-1] + 1
    for i in range(last):
        lifted = work[:, NCOL + i : NCOL + i + 1] * across[:, i : i + 1]
        c_ref[i] = jnp.broadcast_to(lifted, (NCOL, NT))

    def slice_out(a, t):
        here = slab(t)
        values = [fields[i // NRHS][a, i % NRHS, here, :] for i in range(last)]
        for j in columns:
            total = c_ref[0, j : j + 1, :] * values[0]
            for i in range(1, j + 1):
                total = total + c_ref[i, j : j + 1, :] * values[i]
            out_ref[a, j - columns[0], here, :] = total

    return slice_out


def krylov_kernel(
    n_stream,
    n_radial,
    right_hbm,
    diag_hbm,
    face_hbm,
    jac_hbm,
    y0_ref,
    y1_ref,
    y2_ref,
    y3_ref,
    q_ref,
    gram_ref,
    diag_ref,
    face_ref,
    jac_ref,
    w_ref,
    halo_w_ref,
    stage0_ref,
    stage1_ref,
    stage2_ref,
    stage3_ref,
    ahead_ref,
    open_ref,
    slab_ref,
    edge_ref,
    pack_ref,
    acc_ref,
    c_ref,
    first_ref,
    second_ref,
    load_sem,
    halo_send,
    halo_recv,
    first_send,
    first_recv,
    second_send,
    second_recv,
):
    ys = (y0_ref, y1_ref, y2_ref, y3_ref)
    stages = (stage0_ref, stage1_ref, stage2_ref, stage3_ref)
    si = lax.axis_index("stream")
    ri = lax.axis_index("radial")
    core = si % 2
    chip = si // 2
    n_first = 2 * n_radial
    n_second = n_stream // 2
    me_first = ri * 2 + core

    def first_peer(offset):
        other = (me_first + offset) % n_first
        return (chip * 2 + other % 2, other // 2)

    def second_peer(offset):
        return (((chip + offset) % n_second) * 2 + core, ri)

    loads = [
        pltpu.make_async_copy(right_hbm, y0_ref.at[:, :, pl.ds(0, ROWS), :], load_sem.at[0]),
        pltpu.make_async_copy(face_hbm, face_ref, load_sem.at[1]),
        pltpu.make_async_copy(diag_hbm, diag_ref, load_sem.at[2]),
        pltpu.make_async_copy(jac_hbm, jac_ref, load_sem.at[3]),
    ]
    for load in loads:
        load.start()

    barrier = pltpu.get_barrier_semaphore()
    for offset in range(1, n_first):
        pl.semaphore_signal(barrier, inc=1, device_id=first_peer(offset), device_id_type=MESH)
    for offset in range(1, n_second):
        pl.semaphore_signal(barrier, inc=1, device_id=second_peer(offset), device_id_type=MESH)
    peers = ((si + 1, ri), (si - 1, ri), (si, ri + 1), (si, ri - 1))
    present = (si < n_stream - 1, si > 0, ri < n_radial - 1, ri > 0)
    source_of = (1, 0, 3, 2)
    for j in range(4):

        @pl.when(present[j])
        def _(j=j):
            pl.semaphore_signal(barrier, inc=1, device_id=peers[j], device_id_type=MESH)

    loads[3].wait()
    build_operator(jac_ref, w_ref, halo_w_ref)
    for side in range(2):

        @pl.when(jnp.logical_not(present[1 - side]))
        def _(side=side):
            slab_ref[:, side] = jnp.zeros((POWERS, NV, NRHS, LR, NT), jnp.float32)

        @pl.when(jnp.logical_not(present[3 - side]))
        def _(side=side):
            edge_ref[:, side] = jnp.zeros((POWERS, NV, NRHS, LS, NT), jnp.float32)

    greeted = n_first - 1 + n_second - 1
    for j in range(4):
        greeted = greeted + present[j].astype(jnp.int32)
    pl.semaphore_wait(barrier, greeted)

    def halo_copy(k, j):
        if j < 2:
            start = ROWS - LR if j == 0 else 0
            whole = right_hbm if k == 0 else ys[k]
            src = whole.at[:, :, pl.ds(start, LR), :]
            dst = slab_ref.at[k, j]
        else:
            src = pack_ref.at[k, 3 - j]
            dst = edge_ref.at[k, j - 2]
        return pltpu.make_async_remote_copy(
            src_ref=src,
            dst_ref=dst,
            send_sem=halo_send.at[k, j],
            recv_sem=halo_recv.at[k, j],
            device_id=peers[j],
            device_id_type=MESH,
        )

    def send_halo(k, js):
        for j in js:

            @pl.when(present[j])
            def _(j=j):
                halo_copy(k, j).start()

    def wait_halo(k):
        for j in range(4):

            @pl.when(present[source_of[j]])
            def _(j=j):
                halo_copy(k, j).wait_recv()

    send_halo(0, (0, 1))
    loads[0].wait()
    for side in range(2):
        rows = pl.ds(0 if side == 0 else LR - 1, LS, stride=LR)
        for a in range(NV):
            for r in range(NRHS):
                pack_ref[0, side, a, r] = y0_ref[a, r, rows, :]
    send_halo(0, (2, 3))
    loads[1].wait()
    loads[2].wait()
    for a in range(NV):
        diag_ref[a, a] = diag_ref[a, a] - SHIFT

    def spread(round_index, value, slots, send, recv, count, me, peer):
        slots[round_index, me] = value
        copies = []
        for offset in range(1, count):
            copies.append(
                pltpu.make_async_remote_copy(
                    src_ref=slots.at[round_index, me],
                    dst_ref=slots.at[round_index, me],
                    send_sem=send.at[round_index, offset],
                    recv_sem=recv.at[round_index, offset],
                    device_id=peer(offset),
                    device_id_type=MESH,
                )
            )
        for copy in copies:
            copy.start()
        return copies

    def collect(round_index, copies, slots, count):
        for copy in copies:
            copy.wait()
        total = slots[round_index, 0]
        for index in range(1, count):
            total = total + slots[round_index, index]
        return total

    def start_first(index, value):
        return spread(
            index, value, first_ref, first_send, first_recv, n_first, me_first, first_peer
        )

    def start_second(index, copies):
        value = collect(index, copies, first_ref, n_first)
        return spread(
            index, value, second_ref, second_send, second_recv, n_second, chip, second_peer
        )

    acc_ref[...] = jnp.zeros((NCOL, NCOL, 8, NT), jnp.float32)
    pending = None
    for k in range(POWERS):
        scale = RAISE if k == 0 else 1.0
        target = ys[k + 1]
        for j in range(k + 1):
            gram_block(ys[k], ys[j], acc_ref, k, j)
        last = k == POWERS - 1
        if last:
            pending = start_first(0, gram_columns(acc_ref, range(DONE)))
        apply_inner(
            ys[k], target, diag_ref, face_ref, w_ref, stages, ahead_ref, open_ref, scale
        )
        if last:
            pending = start_second(0, pending)
        wait_halo(k)
        add_halo(
            target,
            face_ref,
            halo_w_ref,
            (slab_ref[k, 0], slab_ref[k, 1]),
            (edge_ref[k, 0], edge_ref[k, 1]),
            None if last else pack_ref.at[k + 1],
            scale,
        )
        if not last:
            send_halo(k + 1, range(4))

    for j in range(POWERS + 1):
        gram_block(ys[POWERS], ys[j], acc_ref, POWERS, j)
    final = start_first(1, gram_columns(acc_ref, range(DONE, NCOL)))
    early = collect(0, pending, second_ref, n_second)
    work, across = eliminate(early, DONE)
    slice_out = combine(work, across, ys, c_ref, q_ref, range(DONE))
    final = start_second(1, final)

    def fill(t, carry):
        slice_out(t // LS, t % LS)
        return carry

    lax.fori_loop(0, NV * LS, fill, 0)
    gram_ref[...] = early + collect(1, final, second_ref, n_second)
    for k in range(POWERS):
        for j in range(4):

            @pl.when(present[j])
            def _(k=k, j=j):
                halo_copy(k, j).wait_send()


def krylov(n_stream, n_radial, right, diag, face, jac):
    hbm = pl.BlockSpec(memory_space=pltpu.HBM)
    f32 = jnp.float32
    dma = pltpu.SemaphoreType.DMA
    n_first = 2 * n_radial
    n_second = n_stream // 2
    return pl.pallas_call(
        functools.partial(krylov_kernel, n_stream, n_radial),
        out_shape=(
            *[pltpu.VMEM((NV, NRHS, ROWS + LR, NT), f32)] * (POWERS + 1),
            pltpu.VMEM((NV, DONE, ROWS, NT), f32),
            jax.ShapeDtypeStruct((NCOL, NT), f32),
        ),
        in_specs=[hbm] * 4,
        out_specs=tuple([pl.BlockSpec(memory_space=pltpu.VMEM)] * (POWERS + 3)),
        scratch_shapes=[
            pltpu.VMEM((NV, NV, ROWS, NT), f32),
            pltpu.VMEM((6, ROWS, NT), f32),
            pltpu.SMEM((NV, 6, NV), f32),
            pltpu.VMEM((6 * BLK, KDIM), jnp.bfloat16),
            pltpu.VMEM((4 * BLK, KDIM), jnp.bfloat16),
            pltpu.VMEM((NV, NRHS, LR, NT), f32),
            pltpu.VMEM((NV, NRHS, LR, NT), f32),
            pltpu.VMEM((NV, NRHS, LR, NT), f32),
            pltpu.VMEM((NV, NRHS, LR, NT), f32),
            pltpu.VMEM((NV, NRHS, LR, NT), f32),
            pltpu.VMEM((NV, NRHS, LR, NT), f32),
            pltpu.VMEM((POWERS, 2, NV, NRHS, LR, NT), f32),
            pltpu.VMEM((POWERS, 2, NV, NRHS, LS, NT), f32),
            pltpu.VMEM((POWERS, 2, NV, NRHS, LS, NT), f32),
            pltpu.VMEM((NCOL, NCOL, 8, NT), f32),
            pltpu.VMEM((NCOL, NCOL, NT), f32),
            pltpu.VMEM((2, n_first, NCOL, NT), f32),
            pltpu.VMEM((2, n_second, NCOL, NT), f32),
            dma((4,)),
            dma((POWERS, 4)),
            dma((POWERS, 4)),
            dma((2, n_first)),
            dma((2, n_first)),
            dma((2, n_second)),
            dma((2, n_second)),
        ],
        compiler_params=pltpu.CompilerParams(collective_id=0, has_side_effects=True, vmem_limit_bytes=47_600_000),
    )(right, diag, face, jac)


def basis_kernel(
    gram_ref, y0_ref, y1_ref, y2_ref, y3_ref, early_ref, q_hbm, r_ref, c_ref, late_ref, sem
):
    copies = [
        pltpu.make_async_copy(early_ref.at[a], q_hbm.at[a, pl.ds(0, DONE)], sem.at[0, a])
        for a in range(NV)
    ]
    for copy in copies:
        copy.start()
    work, across = eliminate(gram_ref[...], NCOL)
    row = lax.broadcasted_iota(jnp.int32, (NCOL, NT), 0)
    col = lax.broadcasted_iota(jnp.int32, (NCOL, NT), 1)
    r_ref[...] = jnp.where(row <= col, work, 0.0)[:, :NCOL]
    fields = (y0_ref, y1_ref, y2_ref, y3_ref)
    slice_out = combine(work, across, fields, c_ref, late_ref, range(DONE, NCOL))
    for a in range(NV):

        def fill(t, carry, a=a):
            slice_out(a, t)
            return carry

        lax.fori_loop(0, LS, fill, 0)
        copy = pltpu.make_async_copy(
            late_ref.at[a], q_hbm.at[a, pl.ds(DONE, NCOL - DONE)], sem.at[1, a]
        )
        copy.start()
        copies.append(copy)
    for copy in copies:
        copy.wait()


def basis(gram, early, fields):
    f32 = jnp.float32
    vmem = pl.BlockSpec(memory_space=pltpu.VMEM)
    return pl.pallas_call(
        basis_kernel,
        out_shape=(
            jax.ShapeDtypeStruct((NV, NCOL, ROWS, NT), f32),
            jax.ShapeDtypeStruct((NCOL, NCOL), f32),
        ),
        in_specs=[vmem] * (POWERS + 3),
        out_specs=(pl.BlockSpec(memory_space=pltpu.HBM), vmem),
        scratch_shapes=[
            pltpu.VMEM((NCOL, NCOL, NT), f32),
            pltpu.VMEM((NV, NCOL - DONE, ROWS, NT), f32),
            pltpu.SemaphoreType.DMA((2, NV)),
        ],
        compiler_params=pltpu.CompilerParams(vmem_limit_bytes=24 * 2**20),
    )(gram, *fields, early)


def body(n_stream, n_radial, right_side, diag_block, face_coef, jacobians):
    right = right_side.reshape(NV, NRHS, ROWS, NT)
    diag = diag_block.reshape(NV, NV, ROWS, NT)
    face = face_coef.reshape(6, ROWS, NT)
    jac = jnp.transpose(jacobians, (1, 0, 2))
    *fields, early, gram = krylov(n_stream, n_radial, right, diag, face, jac)
    q, r_factor = basis(gram, early, fields)
    return q.reshape(NV, NCOL, LS, LR, NT), r_factor


def solution(mesh):
    return jax.shard_map(
        functools.partial(body, mesh.shape["stream"], mesh.shape["radial"]),
        mesh=mesh,
        in_specs=(
            P(None, None, "stream", "radial", None),
            P(None, None, "stream", "radial", None),
            P(None, "stream", "radial", None),
            P(),
        ),
        out_specs=(P(None, None, "stream", "radial", None), P()),
        check_vma=False,
    )
```

```python
import functools

import jax
import jax.numpy as jnp
from jax import lax
from jax.experimental import pallas as pl
from jax.experimental.pallas import tpu as pltpu
from jax.sharding import PartitionSpec as P

NV = 5
NRHS = 4
POWERS = 3
NCOL = 16
LS = 16
LR = 16
NT = 128
ROWS = LS * LR
SHIFT = 6.0
BLK = NV * LR
KDIM = 256
OFFSETS = (0, 0, -1, 1, 0, 0)
UNROLL = 4
GRAM_ROWS = 16
GRAM_UNROLL = 8
GRAM_STEPS = ROWS // (GRAM_ROWS * GRAM_UNROLL)
FILL_ROWS = 32
FILL_UNROLL = 2
FILL_STEPS = ROWS // (FILL_ROWS * FILL_UNROLL)
DONE = 12
RAISE = 2.0**24
MESH = pl.DeviceIdType.MESH


def build_operator(jac_ref, w_ref, halo_w_ref):
    col = lax.broadcasted_iota(jnp.int32, (LR, KDIM), 1)
    row = lax.broadcasted_iota(jnp.int32, (LR, KDIM), 0)
    part = col // BLK
    var = (col % BLK) // LR
    cell = col % LR
    masks = {}
    for offset in (-1, 0, 1):
        hit = (cell == row + offset) & (part < 3)
        masks[offset] = [
            jnp.where(hit & (var == b), -1.0, 0.0).astype(jnp.float32) for b in range(NV)
        ]

    def tile(direction, a, offset):
        total = jac_ref[a, direction, 0] * masks[offset][0]
        for b in range(1, NV):
            total = total + jac_ref[a, direction, b] * masks[offset][b]
        head = total.astype(jnp.bfloat16).astype(jnp.float32)
        return jnp.where(part == 1, total - head, head).astype(jnp.bfloat16)

    for a in range(NV):
        for direction, offset in enumerate(OFFSETS):
            start = (a * 6 + direction) * LR
            w_ref[start : start + LR, :] = tile(direction, a, offset)
        for direction in range(4):
            start = direction * BLK + a * LR
            halo_w_ref[start : start + LR, :] = tile(direction, a, 0)


def split_fields(values):
    head = values.astype(jnp.bfloat16)
    tail = (values - head.astype(jnp.float32)).astype(jnp.bfloat16)
    empty = jnp.zeros((KDIM - 3 * BLK, NT), jnp.bfloat16)
    columns = []
    for r in range(NRHS):
        head_r = head[:, r].reshape(BLK, NT)
        tail_r = tail[:, r].reshape(BLK, NT)
        columns.append(jnp.concatenate([head_r, head_r, tail_r, empty], axis=0))
    return jnp.concatenate(columns, axis=1)


def slab(s):
    return pl.ds(pl.multiple_of(s * LR, LR), LR)


def apply_blocks(source, diag_ref, stage, s, scale):
    for half in range(2):
        rows = pl.ds(pl.multiple_of(s * LR + half * 8, 8), 8)
        fields = [[source[b, r, rows, :] for r in range(NRHS)] for b in range(NV)]
        for a in range(NV):
            totals = [None] * NRHS
            for b in range(NV):
                block = diag_ref[a, b, rows, :]
                if scale != 1.0:
                    block = block * scale
                for r in range(NRHS):
                    term = block * fields[b][r]
                    totals[r] = term if b == 0 else totals[r] + term
            for r in range(NRHS):
                stage[a, r, half * 8 : half * 8 + 8, :] = totals[r]


def apply_inner(source, target, diag_ref, face_ref, w_ref, stages, ahead_ref, open_ref, scale):
    cells = [(a, r) for a in range(NV) for r in range(NRHS)]
    ahead_ref[...] = jnp.zeros((NV, NRHS, LR, NT), jnp.float32)
    open_ref[...] = jnp.zeros((NV, NRHS, LR, NT), jnp.float32)

    def step(t, carry):
        s0 = t * UNROLL
        for u in range(UNROLL):
            apply_blocks(source, diag_ref, stages[u], s0 + u, scale)
        ahead = {cell: ahead_ref[cell[0], cell[1]] for cell in cells}
        unfinished = {cell: open_ref[cell[0], cell[1]] for cell in cells}
        for u in range(UNROLL):
            s = s0 + u
            before = jnp.where(s == 0, LS, s - 1) if u == 0 else s - 1
            product = jnp.dot(
                w_ref[...],
                split_fields(source[:, :, slab(s), :]),
                preferred_element_type=jnp.float32,
            )
            face = [face_ref[0, slab(jnp.minimum(s + 1, LS - 1)), :]]
            face.append(face_ref[1, slab(jnp.maximum(s - 1, 0)), :])
            face += [face_ref[d, slab(s), :] for d in range(2, 6)]
            if scale != 1.0:
                face = [weight * scale for weight in face]
            for a, r in cells:

                def part(d, a=a, r=r):
                    start = (a * 6 + d) * LR
                    return product[start : start + LR, r * NT : (r + 1) * NT]

                target[a, r, slab(before), :] = unfinished[a, r] + face[1] * part(1)
                total = face[2] * part(2) + face[3] * part(3)
                total = total + face[4] * pltpu.roll(part(4), 1, 1)
                total = total + face[5] * pltpu.roll(part(5), NT - 1, 1)
                unfinished[a, r] = total + (stages[u][a, r] + ahead[a, r])
                ahead[a, r] = face[0] * part(0)
        for a, r in cells:
            ahead_ref[a, r] = ahead[a, r]
            open_ref[a, r] = unfinished[a, r]
        return carry

    lax.fori_loop(0, LS // UNROLL, step, 0)
    target[:, :, ROWS - LR : ROWS, :] = open_ref[...]


def add_halo(target, face_ref, halo_w_ref, slabs, edges, rows_ref, scale):
    for side in range(2):
        start = 0 if side == 0 else ROWS - LR
        product = jnp.dot(
            halo_w_ref[side * BLK : (side + 1) * BLK, :],
            split_fields(slabs[side]),
            preferred_element_type=jnp.float32,
        )
        weight = face_ref[side, start : start + LR, :] * scale
        for a in range(NV):
            for r in range(NRHS):
                target[a, r, start : start + LR, :] = target[a, r, start : start + LR, :] + (
                    weight * product[a * LR : (a + 1) * LR, r * NT : (r + 1) * NT]
                )
    for side in range(2):
        rows = pl.ds(0 if side == 0 else LR - 1, LS, stride=LR)
        product = jnp.dot(
            halo_w_ref[(2 + side) * BLK : (3 + side) * BLK, :],
            split_fields(edges[side]),
            preferred_element_type=jnp.float32,
        )
        weight = face_ref[2 + side, rows, :] * scale
        for a in range(NV):
            for r in range(NRHS):
                fresh = target[a, r, rows, :] + weight * (
                    product[a * LR : (a + 1) * LR, r * NT : (r + 1) * NT]
                )
                target[a, r, rows, :] = fresh
                if rows_ref is not None:
                    rows_ref[side, a, r] = fresh


def gram_block(left, right, acc_ref, k, j):
    pairs = [(p, q) for p in range(NRHS) for q in range(NRHS) if k != j or q <= p]

    def step(t, sums):
        a = t // GRAM_STEPS
        sums = list(sums)
        for u in range(GRAM_UNROLL):
            start = ((t % GRAM_STEPS) * GRAM_UNROLL + u) * GRAM_ROWS
            rows = pl.ds(pl.multiple_of(start, GRAM_ROWS), GRAM_ROWS)
            mine = [left[a, p, rows, :] for p in range(NRHS)]
            other = mine if k == j else [right[a, q, rows, :] for q in range(NRHS)]
            for index, (p, q) in enumerate(pairs):
                term = mine[p] * other[q]
                for piece in range(GRAM_ROWS // 8):
                    sums[index] = sums[index] + term[piece * 8 : piece * 8 + 8]
        return tuple(sums)

    empty = tuple(jnp.zeros((8, NT), jnp.float32) for _ in pairs)
    sums = lax.fori_loop(0, NV * GRAM_STEPS, step, empty)
    for index, (p, q) in enumerate(pairs):
        acc_ref[4 * k + p, 4 * j + q] = sums[index]
        if k == j and p != q:
            acc_ref[4 * k + q, 4 * j + p] = sums[index]


def gram_columns(acc_ref, columns):
    lane = lax.broadcasted_iota(jnp.int32, (NCOL, NT), 1)
    table = jnp.zeros((NCOL, NT), jnp.float32)
    for i in columns:
        rows = jnp.sum(acc_ref[i], axis=1)
        table = table + jnp.where(lane == i, jnp.sum(rows, axis=1, keepdims=True), 0.0)
    return table


def eliminate(table, count):
    row = lax.broadcasted_iota(jnp.int32, (NCOL, NT), 0)
    col = lax.broadcasted_iota(jnp.int32, (NCOL, NT), 1)
    square = table[:, :NCOL]
    flipped = jnp.concatenate([square.T, jnp.zeros((NCOL, NT - NCOL), jnp.float32)], axis=1)
    gram = jnp.where((row // NRHS > col // NRHS) & (col < NCOL), flipped, table)
    on_diag = jnp.where(row == col, gram, 0.0)
    down = jnp.sum(on_diag, axis=1, keepdims=True)
    across = jnp.sum(on_diag, axis=0, keepdims=True)
    down = 1.0 / jnp.sqrt(jnp.where(row[:, :1] < count, down, 1.0))
    across = 1.0 / jnp.sqrt(jnp.where(col[:1] < count, across, 1.0))
    work = gram * down * across
    work = jnp.where(col == row + NCOL, 1.0, work)
    for i in range(count):
        lead = work[:, i : i + 1]
        root = 1.0 / jnp.sqrt(work[i : i + 1, i : i + 1])
        line = work[i : i + 1, :] * root
        work = jnp.where(row == i, line, jnp.where(row > i, work - (lead * root) * line, work))
    return work, across


def combine(work, across, fields, c_ref, out_ref, columns):
    last = columns[-1] + 1
    for i in range(last):
        lifted = work[:, NCOL + i : NCOL + i + 1] * across[:, i : i + 1]
        c_ref[i] = jnp.broadcast_to(lifted, (NCOL, NT))

    def slice_out(a, t):
        for u in range(FILL_UNROLL):
            part_out(a, (t * FILL_UNROLL + u) * FILL_ROWS)

    def part_out(a, start):
        here = pl.ds(pl.multiple_of(start, FILL_ROWS), FILL_ROWS)
        values = [fields[i // NRHS][a, i % NRHS, here, :] for i in range(last)]
        for j in columns:
            total = c_ref[0, j : j + 1, :] * values[0]
            for i in range(1, j + 1):
                total = total + c_ref[i, j : j + 1, :] * values[i]
            out_ref[a, j - columns[0], here, :] = total

    return slice_out


def krylov_kernel(
    n_stream,
    n_radial,
    right_hbm,
    diag_hbm,
    face_hbm,
    jac_hbm,
    y0_ref,
    y1_ref,
    y2_ref,
    y3_ref,
    q_ref,
    gram_ref,
    diag_ref,
    face_ref,
    jac_ref,
    w_ref,
    halo_w_ref,
    stage0_ref,
    stage1_ref,
    stage2_ref,
    stage3_ref,
    ahead_ref,
    open_ref,
    slab_ref,
    edge_ref,
    pack_ref,
    acc_ref,
    c_ref,
    first_ref,
    second_ref,
    load_sem,
    halo_send,
    halo_recv,
    first_send,
    first_recv,
    second_send,
    second_recv,
):
    ys = (y0_ref, y1_ref, y2_ref, y3_ref)
    stages = (stage0_ref, stage1_ref, stage2_ref, stage3_ref)
    si = lax.axis_index("stream")
    ri = lax.axis_index("radial")
    core = si % 2
    chip = si // 2
    n_first = 2 * n_radial
    n_second = n_stream // 2
    me_first = ri * 2 + core

    def first_peer(offset):
        other = (me_first + offset) % n_first
        return (chip * 2 + other % 2, other // 2)

    def second_peer(offset):
        return (((chip + offset) % n_second) * 2 + core, ri)

    loads = [
        pltpu.make_async_copy(right_hbm, y0_ref.at[:, :, pl.ds(0, ROWS), :], load_sem.at[0]),
        pltpu.make_async_copy(face_hbm, face_ref, load_sem.at[1]),
        pltpu.make_async_copy(diag_hbm, diag_ref, load_sem.at[2]),
        pltpu.make_async_copy(jac_hbm, jac_ref, load_sem.at[3]),
    ]
    for load in loads:
        load.start()

    barrier = pltpu.get_barrier_semaphore()
    for offset in range(1, n_first):
        pl.semaphore_signal(barrier, inc=1, device_id=first_peer(offset), device_id_type=MESH)
    for offset in range(1, n_second):
        pl.semaphore_signal(barrier, inc=1, device_id=second_peer(offset), device_id_type=MESH)
    peers = ((si + 1, ri), (si - 1, ri), (si, ri + 1), (si, ri - 1))
    present = (si < n_stream - 1, si > 0, ri < n_radial - 1, ri > 0)
    source_of = (1, 0, 3, 2)
    for j in range(4):

        @pl.when(present[j])
        def _(j=j):
            pl.semaphore_signal(barrier, inc=1, device_id=peers[j], device_id_type=MESH)

    loads[3].wait()
    build_operator(jac_ref, w_ref, halo_w_ref)
    for side in range(2):

        @pl.when(jnp.logical_not(present[1 - side]))
        def _(side=side):
            slab_ref[:, side] = jnp.zeros((POWERS, NV, NRHS, LR, NT), jnp.float32)

        @pl.when(jnp.logical_not(present[3 - side]))
        def _(side=side):
            edge_ref[:, side] = jnp.zeros((POWERS, NV, NRHS, LS, NT), jnp.float32)

    greeted = n_first - 1 + n_second - 1
    for j in range(4):
        greeted = greeted + present[j].astype(jnp.int32)
    pl.semaphore_wait(barrier, greeted)

    def halo_copy(k, j):
        if j < 2:
            start = ROWS - LR if j == 0 else 0
            whole = right_hbm if k == 0 else ys[k]
            src = whole.at[:, :, pl.ds(start, LR), :]
            dst = slab_ref.at[k, j]
        else:
            src = pack_ref.at[k, 3 - j]
            dst = edge_ref.at[k, j - 2]
        return pltpu.make_async_remote_copy(
            src_ref=src,
            dst_ref=dst,
            send_sem=halo_send.at[k, j],
            recv_sem=halo_recv.at[k, j],
            device_id=peers[j],
            device_id_type=MESH,
        )

    def send_halo(k, js):
        for j in js:

            @pl.when(present[j])
            def _(j=j):
                halo_copy(k, j).start()

    def wait_halo(k):
        for j in range(4):

            @pl.when(present[source_of[j]])
            def _(j=j):
                halo_copy(k, j).wait_recv()

    send_halo(0, (0, 1))
    loads[0].wait()
    for side in range(2):
        rows = pl.ds(0 if side == 0 else LR - 1, LS, stride=LR)
        for a in range(NV):
            for r in range(NRHS):
                pack_ref[0, side, a, r] = y0_ref[a, r, rows, :]
    send_halo(0, (2, 3))
    acc_ref[...] = jnp.zeros((NCOL, NCOL, 8, NT), jnp.float32)
    gram_block(y0_ref, y0_ref, acc_ref, 0, 0)
    loads[1].wait()
    loads[2].wait()
    for a in range(NV):
        diag_ref[a, a] = diag_ref[a, a] - SHIFT

    def spread(round_index, value, slots, send, recv, count, me, peer):
        slots[round_index, me] = value
        copies = []
        for offset in range(1, count):
            copies.append(
                pltpu.make_async_remote_copy(
                    src_ref=slots.at[round_index, me],
                    dst_ref=slots.at[round_index, me],
                    send_sem=send.at[round_index, offset],
                    recv_sem=recv.at[round_index, offset],
                    device_id=peer(offset),
                    device_id_type=MESH,
                )
            )
        for copy in copies:
            copy.start()
        return copies

    def collect(round_index, copies, slots, count):
        for copy in copies:
            copy.wait()
        total = slots[round_index, 0]
        for index in range(1, count):
            total = total + slots[round_index, index]
        return total

    def start_first(index, value):
        return spread(
            index, value, first_ref, first_send, first_recv, n_first, me_first, first_peer
        )

    def start_second(index, copies):
        value = collect(index, copies, first_ref, n_first)
        return spread(
            index, value, second_ref, second_send, second_recv, n_second, chip, second_peer
        )

    pending = None
    for k in range(POWERS):
        scale = RAISE if k == 0 else 1.0
        target = ys[k + 1]
        for j in range(k + 1 if k else 0):
            gram_block(ys[k], ys[j], acc_ref, k, j)
        last = k == POWERS - 1
        if last:
            pending = start_first(0, gram_columns(acc_ref, range(DONE)))
        apply_inner(
            ys[k], target, diag_ref, face_ref, w_ref, stages, ahead_ref, open_ref, scale
        )
        if last:
            pending = start_second(0, pending)
        wait_halo(k)
        add_halo(
            target,
            face_ref,
            halo_w_ref,
            (slab_ref[k, 0], slab_ref[k, 1]),
            (edge_ref[k, 0], edge_ref[k, 1]),
            None if last else pack_ref.at[k + 1],
            scale,
        )
        if not last:
            send_halo(k + 1, range(4))

    for j in range(POWERS + 1):
        gram_block(ys[POWERS], ys[j], acc_ref, POWERS, j)
    final = start_first(1, gram_columns(acc_ref, range(DONE, NCOL)))
    early = collect(0, pending, second_ref, n_second)
    work, across = eliminate(early, DONE)
    slice_out = combine(work, across, ys, c_ref, q_ref, range(DONE))
    final = start_second(1, final)

    def fill(t, carry):
        slice_out(t // FILL_STEPS, t % FILL_STEPS)
        return carry

    lax.fori_loop(0, NV * FILL_STEPS, fill, 0)
    gram_ref[...] = early + collect(1, final, second_ref, n_second)
    for k in range(POWERS):
        for j in range(4):

            @pl.when(present[j])
            def _(k=k, j=j):
                halo_copy(k, j).wait_send()


def krylov(n_stream, n_radial, right, diag, face, jac):
    hbm = pl.BlockSpec(memory_space=pltpu.HBM)
    f32 = jnp.float32
    dma = pltpu.SemaphoreType.DMA
    n_first = 2 * n_radial
    n_second = n_stream // 2
    return pl.pallas_call(
        functools.partial(krylov_kernel, n_stream, n_radial),
        out_shape=(
            *[pltpu.VMEM((NV, NRHS, ROWS + LR, NT), f32)] * (POWERS + 1),
            pltpu.VMEM((NV, DONE, ROWS, NT), f32),
            pltpu.VMEM((NCOL, NT), f32),
        ),
        in_specs=[hbm] * 4,
        out_specs=tuple([pl.BlockSpec(memory_space=pltpu.VMEM)] * (POWERS + 3)),
        scratch_shapes=[
            pltpu.VMEM((NV, NV, ROWS, NT), f32),
            pltpu.VMEM((6, ROWS, NT), f32),
            pltpu.SMEM((NV, 6, NV), f32),
            pltpu.VMEM((6 * BLK, KDIM), jnp.bfloat16),
            pltpu.VMEM((4 * BLK, KDIM), jnp.bfloat16),
            pltpu.VMEM((NV, NRHS, LR, NT), f32),
            pltpu.VMEM((NV, NRHS, LR, NT), f32),
            pltpu.VMEM((NV, NRHS, LR, NT), f32),
            pltpu.VMEM((NV, NRHS, LR, NT), f32),
            pltpu.VMEM((NV, NRHS, LR, NT), f32),
            pltpu.VMEM((NV, NRHS, LR, NT), f32),
            pltpu.VMEM((POWERS, 2, NV, NRHS, LR, NT), f32),
            pltpu.VMEM((POWERS, 2, NV, NRHS, LS, NT), f32),
            pltpu.VMEM((POWERS, 2, NV, NRHS, LS, NT), f32),
            pltpu.VMEM((NCOL, NCOL, 8, NT), f32),
            pltpu.VMEM((NCOL, NCOL, NT), f32),
            pltpu.VMEM((2, n_first, NCOL, NT), f32),
            pltpu.VMEM((2, n_second, NCOL, NT), f32),
            dma((4,)),
            dma((POWERS, 4)),
            dma((POWERS, 4)),
            dma((2, n_first)),
            dma((2, n_first)),
            dma((2, n_second)),
            dma((2, n_second)),
        ],
        compiler_params=pltpu.CompilerParams(collective_id=0, has_side_effects=True, vmem_limit_bytes=47_600_000),
    )(right, diag, face, jac)


def basis_kernel(
    gram_ref, y0_ref, y1_ref, y2_ref, y3_ref, early_ref, q_hbm, r_ref, c_ref, late_ref, sem
):
    copies = [
        pltpu.make_async_copy(early_ref.at[a], q_hbm.at[a, pl.ds(0, DONE)], sem.at[0, a])
        for a in range(NV)
    ]
    for copy in copies:
        copy.start()
    work, across = eliminate(gram_ref[...], NCOL)
    row = lax.broadcasted_iota(jnp.int32, (NCOL, NT), 0)
    col = lax.broadcasted_iota(jnp.int32, (NCOL, NT), 1)
    r_ref[...] = jnp.where(row <= col, work, 0.0)[:, :NCOL]
    fields = (y0_ref, y1_ref, y2_ref, y3_ref)
    slice_out = combine(work, across, fields, c_ref, late_ref, range(DONE, NCOL))
    for a in range(NV):

        def fill(t, carry, a=a):
            slice_out(a, t)
            return carry

        lax.fori_loop(0, FILL_STEPS, fill, 0)
        copy = pltpu.make_async_copy(
            late_ref.at[a], q_hbm.at[a, pl.ds(DONE, NCOL - DONE)], sem.at[1, a]
        )
        copy.start()
        copies.append(copy)
    for copy in copies:
        copy.wait()


def basis(gram, early, fields):
    f32 = jnp.float32
    vmem = pl.BlockSpec(memory_space=pltpu.VMEM)
    return pl.pallas_call(
        basis_kernel,
        out_shape=(
            jax.ShapeDtypeStruct((NV, NCOL, ROWS, NT), f32),
            jax.ShapeDtypeStruct((NCOL, NCOL), f32),
        ),
        in_specs=[vmem] * (POWERS + 3),
        out_specs=(pl.BlockSpec(memory_space=pltpu.HBM), vmem),
        scratch_shapes=[
            pltpu.VMEM((NCOL, NCOL, NT), f32),
            pltpu.VMEM((NV, NCOL - DONE, ROWS, NT), f32),
            pltpu.SemaphoreType.DMA((2, NV)),
        ],
        compiler_params=pltpu.CompilerParams(vmem_limit_bytes=24 * 2**20),
    )(gram, *fields, early)


def body(n_stream, n_radial, right_side, diag_block, face_coef, jacobians):
    right = right_side.reshape(NV, NRHS, ROWS, NT)
    diag = diag_block.reshape(NV, NV, ROWS, NT)
    face = face_coef.reshape(6, ROWS, NT)
    jac = jnp.transpose(jacobians, (1, 0, 2))
    *fields, early, gram = krylov(n_stream, n_radial, right, diag, face, jac)
    q, r_factor = basis(gram, early, fields)
    return q.reshape(NV, NCOL, LS, LR, NT), r_factor


def solution(mesh):
    return jax.shard_map(
        functools.partial(body, mesh.shape["stream"], mesh.shape["radial"]),
        mesh=mesh,
        in_specs=(
            P(None, None, "stream", "radial", None),
            P(None, None, "stream", "radial", None),
            P(None, "stream", "radial", None),
            P(),
        ),
        out_specs=(P(None, None, "stream", "radial", None), P()),
        check_vma=False,
    )
```

```python
import functools

import jax
import jax.numpy as jnp
from jax import lax
from jax.experimental import pallas as pl
from jax.experimental.pallas import tpu as pltpu
from jax.sharding import PartitionSpec as P

NV = 5
NRHS = 4
POWERS = 3
NCOL = 16
LS = 16
LR = 16
NT = 128
ROWS = LS * LR
SHIFT = 6.0
BLK = NV * LR
KDIM = 256
OFFSETS = (0, 0, -1, 1, 0, 0)
UNROLL = 4
DIAG_ROWS = UNROLL * LR
GRAM_ROWS = 16
GRAM_UNROLL = 8
GRAM_STEPS = ROWS // (GRAM_ROWS * GRAM_UNROLL)
FILL_ROWS = 32
FILL_UNROLL = 2
FILL_STEPS = ROWS // (FILL_ROWS * FILL_UNROLL)
DONE = 12
RAISE = 2.0**24
MESH = pl.DeviceIdType.MESH


def build_operator(jac_ref, w_ref, halo_w_ref):
    col = lax.broadcasted_iota(jnp.int32, (LR, KDIM), 1)
    row = lax.broadcasted_iota(jnp.int32, (LR, KDIM), 0)
    part = col // BLK
    var = (col % BLK) // LR
    cell = col % LR
    masks = {}
    for offset in (-1, 0, 1):
        hit = (cell == row + offset) & (part < 3)
        masks[offset] = [
            jnp.where(hit & (var == b), -1.0, 0.0).astype(jnp.float32) for b in range(NV)
        ]

    def tile(direction, a, offset):
        total = jac_ref[a, direction, 0] * masks[offset][0]
        for b in range(1, NV):
            total = total + jac_ref[a, direction, b] * masks[offset][b]
        head = total.astype(jnp.bfloat16).astype(jnp.float32)
        return jnp.where(part == 1, total - head, head).astype(jnp.bfloat16)

    for a in range(NV):
        for direction, offset in enumerate(OFFSETS):
            start = (a * 6 + direction) * LR
            w_ref[start : start + LR, :] = tile(direction, a, offset)
        for direction in range(4):
            start = direction * BLK + a * LR
            halo_w_ref[start : start + LR, :] = tile(direction, a, 0)


def split_fields(values):
    head = values.astype(jnp.bfloat16)
    tail = (values - head.astype(jnp.float32)).astype(jnp.bfloat16)
    empty = jnp.zeros((KDIM - 3 * BLK, NT), jnp.bfloat16)
    columns = []
    for r in range(NRHS):
        head_r = head[:, r].reshape(BLK, NT)
        tail_r = tail[:, r].reshape(BLK, NT)
        columns.append(jnp.concatenate([head_r, head_r, tail_r, empty], axis=0))
    return jnp.concatenate(columns, axis=1)


def slab(s):
    return pl.ds(pl.multiple_of(s * LR, LR), LR)


def apply_blocks(source, diag_ref, stage, s, scale):
    for half in range(2):
        rows = pl.ds(pl.multiple_of(s * LR + half * 8, 8), 8)
        fields = [[source[b, r, rows, :] for r in range(NRHS)] for b in range(NV)]
        for a in range(NV):
            totals = [None] * NRHS
            for b in range(NV):
                block = diag_ref[a, b, rows, :]
                if scale != 1.0:
                    block = block * scale
                for r in range(NRHS):
                    term = block * fields[b][r]
                    totals[r] = term if b == 0 else totals[r] + term
            for r in range(NRHS):
                stage[a, r, half * 8 : half * 8 + 8, :] = totals[r]


def apply_inner(
    source, target, diag_ref, face_ref, w_ref, stages, ahead_ref, open_ref, scale, prepare=None
):
    cells = [(a, r) for a in range(NV) for r in range(NRHS)]
    ahead_ref[...] = jnp.zeros((NV, NRHS, LR, NT), jnp.float32)
    open_ref[...] = jnp.zeros((NV, NRHS, LR, NT), jnp.float32)

    def step(t, carry):
        s0 = t * UNROLL
        if prepare is not None:
            prepare(t)
        for u in range(UNROLL):
            apply_blocks(source, diag_ref, stages[u], s0 + u, scale)
        ahead = {cell: ahead_ref[cell[0], cell[1]] for cell in cells}
        unfinished = {cell: open_ref[cell[0], cell[1]] for cell in cells}
        for u in range(UNROLL):
            s = s0 + u
            before = jnp.where(s == 0, LS, s - 1) if u == 0 else s - 1
            product = jnp.dot(
                w_ref[...],
                split_fields(source[:, :, slab(s), :]),
                preferred_element_type=jnp.float32,
            )
            face = [face_ref[0, slab(jnp.minimum(s + 1, LS - 1)), :]]
            face.append(face_ref[1, slab(jnp.maximum(s - 1, 0)), :])
            face += [face_ref[d, slab(s), :] for d in range(2, 6)]
            if scale != 1.0:
                face = [weight * scale for weight in face]
            for a, r in cells:

                def part(d, a=a, r=r):
                    start = (a * 6 + d) * LR
                    return product[start : start + LR, r * NT : (r + 1) * NT]

                target[a, r, slab(before), :] = unfinished[a, r] + face[1] * part(1)
                total = face[2] * part(2) + face[3] * part(3)
                total = total + face[4] * pltpu.roll(part(4), 1, 1)
                total = total + face[5] * pltpu.roll(part(5), NT - 1, 1)
                unfinished[a, r] = total + (stages[u][a, r] + ahead[a, r])
                ahead[a, r] = face[0] * part(0)
        for a, r in cells:
            ahead_ref[a, r] = ahead[a, r]
            open_ref[a, r] = unfinished[a, r]
        return carry

    lax.fori_loop(0, LS // UNROLL, step, 0)
    target[:, :, ROWS - LR : ROWS, :] = open_ref[...]


def add_halo(target, face_ref, halo_w_ref, slabs, edges, rows_ref, scale):
    for side in range(2):
        start = 0 if side == 0 else ROWS - LR
        product = jnp.dot(
            halo_w_ref[side * BLK : (side + 1) * BLK, :],
            split_fields(slabs[side]),
            preferred_element_type=jnp.float32,
        )
        weight = face_ref[side, start : start + LR, :] * scale
        for a in range(NV):
            for r in range(NRHS):
                target[a, r, start : start + LR, :] = target[a, r, start : start + LR, :] + (
                    weight * product[a * LR : (a + 1) * LR, r * NT : (r + 1) * NT]
                )
    for side in range(2):
        rows = pl.ds(0 if side == 0 else LR - 1, LS, stride=LR)
        product = jnp.dot(
            halo_w_ref[(2 + side) * BLK : (3 + side) * BLK, :],
            split_fields(edges[side]),
            preferred_element_type=jnp.float32,
        )
        weight = face_ref[2 + side, rows, :] * scale
        for a in range(NV):
            for r in range(NRHS):
                fresh = target[a, r, rows, :] + weight * (
                    product[a * LR : (a + 1) * LR, r * NT : (r + 1) * NT]
                )
                target[a, r, rows, :] = fresh
                if rows_ref is not None:
                    rows_ref[side, a, r] = fresh


def gram_block(left, right, acc_ref, k, j):
    pairs = [(p, q) for p in range(NRHS) for q in range(NRHS) if k != j or q <= p]

    def step(t, sums):
        a = t // GRAM_STEPS
        sums = list(sums)
        for u in range(GRAM_UNROLL):
            start = ((t % GRAM_STEPS) * GRAM_UNROLL + u) * GRAM_ROWS
            rows = pl.ds(pl.multiple_of(start, GRAM_ROWS), GRAM_ROWS)
            mine = [left[a, p, rows, :] for p in range(NRHS)]
            other = mine if k == j else [right[a, q, rows, :] for q in range(NRHS)]
            for index, (p, q) in enumerate(pairs):
                term = mine[p] * other[q]
                for piece in range(GRAM_ROWS // 8):
                    sums[index] = sums[index] + term[piece * 8 : piece * 8 + 8]
        return tuple(sums)

    empty = tuple(jnp.zeros((8, NT), jnp.float32) for _ in pairs)
    sums = lax.fori_loop(0, NV * GRAM_STEPS, step, empty)
    for index, (p, q) in enumerate(pairs):
        acc_ref[4 * k + p, 4 * j + q] = sums[index]
        if k == j and p != q:
            acc_ref[4 * k + q, 4 * j + p] = sums[index]


def gram_columns(acc_ref, columns):
    lane = lax.broadcasted_iota(jnp.int32, (NCOL, NT), 1)
    table = jnp.zeros((NCOL, NT), jnp.float32)
    for i in columns:
        rows = jnp.sum(acc_ref[i], axis=1)
        table = table + jnp.where(lane == i, jnp.sum(rows, axis=1, keepdims=True), 0.0)
    return table


def eliminate(table, count):
    row = lax.broadcasted_iota(jnp.int32, (NCOL, NT), 0)
    col = lax.broadcasted_iota(jnp.int32, (NCOL, NT), 1)
    square = table[:, :NCOL]
    flipped = jnp.concatenate([square.T, jnp.zeros((NCOL, NT - NCOL), jnp.float32)], axis=1)
    gram = jnp.where((row // NRHS > col // NRHS) & (col < NCOL), flipped, table)
    on_diag = jnp.where(row == col, gram, 0.0)
    down = jnp.sum(on_diag, axis=1, keepdims=True)
    across = jnp.sum(on_diag, axis=0, keepdims=True)
    down = 1.0 / jnp.sqrt(jnp.where(row[:, :1] < count, down, 1.0))
    across = 1.0 / jnp.sqrt(jnp.where(col[:1] < count, across, 1.0))
    work = gram * down * across
    work = jnp.where(col == row + NCOL, 1.0, work)
    for i in range(count):
        line = work[i : i + 1, :] * (1.0 / work[i : i + 1, i : i + 1])
        work = jnp.where(row > i, work - work[:, i : i + 1] * line, work)
    pivots = jnp.sum(jnp.where(row == col, work, 0.0), axis=1, keepdims=True)
    work = work * (1.0 / jnp.sqrt(jnp.where(row[:, :1] < count, pivots, 1.0)))
    return work, across


def combine(work, across, fields, c_ref, out_ref, columns):
    last = columns[-1] + 1
    for i in range(last):
        lifted = work[:, NCOL + i : NCOL + i + 1] * across[:, i : i + 1]
        c_ref[i] = jnp.broadcast_to(lifted, (NCOL, NT))

    def slice_out(a, t):
        for u in range(FILL_UNROLL):
            part_out(a, (t * FILL_UNROLL + u) * FILL_ROWS)

    def part_out(a, start):
        here = pl.ds(pl.multiple_of(start, FILL_ROWS), FILL_ROWS)
        values = [fields[i // NRHS][a, i % NRHS, here, :] for i in range(last)]
        for j in columns:
            total = c_ref[0, j : j + 1, :] * values[0]
            for i in range(1, j + 1):
                total = total + c_ref[i, j : j + 1, :] * values[i]
            out_ref[a, j - columns[0], here, :] = total

    return slice_out


def krylov_kernel(
    n_stream,
    n_radial,
    right_hbm,
    diag_hbm,
    face_hbm,
    jac_hbm,
    y0_ref,
    y1_ref,
    y2_ref,
    y3_ref,
    q_ref,
    gram_ref,
    diag_ref,
    face_ref,
    jac_ref,
    w_ref,
    halo_w_ref,
    stage0_ref,
    stage1_ref,
    stage2_ref,
    stage3_ref,
    ahead_ref,
    open_ref,
    slab_ref,
    edge_ref,
    pack_ref,
    acc_ref,
    c_ref,
    first_ref,
    second_ref,
    load_sem,
    halo_send,
    halo_recv,
    first_send,
    first_recv,
    second_send,
    second_recv,
):
    ys = (y0_ref, y1_ref, y2_ref, y3_ref)
    stages = (stage0_ref, stage1_ref, stage2_ref, stage3_ref)
    si = lax.axis_index("stream")
    ri = lax.axis_index("radial")
    core = si % 2
    chip = si // 2
    n_first = 2 * n_radial
    n_second = n_stream // 2
    me_first = ri * 2 + core

    def first_peer(offset):
        other = (me_first + offset) % n_first
        return (chip * 2 + other % 2, other // 2)

    def second_peer(offset):
        return (((chip + offset) % n_second) * 2 + core, ri)

    loads = [
        pltpu.make_async_copy(right_hbm, y0_ref.at[:, :, pl.ds(0, ROWS), :], load_sem.at[0]),
        pltpu.make_async_copy(face_hbm, face_ref, load_sem.at[1]),
        pltpu.make_async_copy(jac_hbm, jac_ref, load_sem.at[2]),
    ]

    def diag_load(t):
        rows = pl.ds(pl.multiple_of(t * DIAG_ROWS, DIAG_ROWS), DIAG_ROWS)
        return pltpu.make_async_copy(
            diag_hbm.at[:, :, rows, :], diag_ref.at[:, :, rows, :], load_sem.at[3 + t]
        )

    def diag_ready(t):
        rows = pl.ds(pl.multiple_of(t * DIAG_ROWS, DIAG_ROWS), DIAG_ROWS)
        diag_load(t).wait()
        for a in range(NV):
            diag_ref[a, a, rows, :] = diag_ref[a, a, rows, :] - SHIFT

    loads[2].start()
    loads[0].start()
    loads[1].start()
    for t in range(LS // UNROLL):
        diag_load(t).start()

    barrier = pltpu.get_barrier_semaphore()
    peers = ((si + 1, ri), (si - 1, ri), (si, ri + 1), (si, ri - 1))
    present = (si < n_stream - 1, si > 0, ri < n_radial - 1, ri > 0)
    source_of = (1, 0, 3, 2)
    for j in range(4):

        @pl.when(present[j])
        def _(j=j):
            pl.semaphore_signal(barrier, inc=1, device_id=peers[j], device_id_type=MESH)

    for offset in range(1, n_first):
        pl.semaphore_signal(barrier, inc=1, device_id=first_peer(offset), device_id_type=MESH)
    for offset in range(1, n_second):
        pl.semaphore_signal(barrier, inc=1, device_id=second_peer(offset), device_id_type=MESH)
    loads[2].wait()
    build_operator(jac_ref, w_ref, halo_w_ref)
    for side in range(2):

        @pl.when(jnp.logical_not(present[1 - side]))
        def _(side=side):
            slab_ref[:, side] = jnp.zeros((POWERS, NV, NRHS, LR, NT), jnp.float32)

        @pl.when(jnp.logical_not(present[3 - side]))
        def _(side=side):
            edge_ref[:, side] = jnp.zeros((POWERS, NV, NRHS, LS, NT), jnp.float32)

    greeted = n_first - 1 + n_second - 1
    for j in range(4):
        greeted = greeted + present[j].astype(jnp.int32)
    pl.semaphore_wait(barrier, greeted)

    def halo_copy(k, j):
        if j < 2:
            start = ROWS - LR if j == 0 else 0
            whole = right_hbm if k == 0 else ys[k]
            src = whole.at[:, :, pl.ds(start, LR), :]
            dst = slab_ref.at[k, j]
        else:
            src = pack_ref.at[k, 3 - j]
            dst = edge_ref.at[k, j - 2]
        return pltpu.make_async_remote_copy(
            src_ref=src,
            dst_ref=dst,
            send_sem=halo_send.at[k, j],
            recv_sem=halo_recv.at[k, j],
            device_id=peers[j],
            device_id_type=MESH,
        )

    def send_halo(k, js):
        for j in js:

            @pl.when(present[j])
            def _(j=j):
                halo_copy(k, j).start()

    def wait_halo(k):
        for j in range(4):

            @pl.when(present[source_of[j]])
            def _(j=j):
                halo_copy(k, j).wait_recv()

    send_halo(0, (0, 1))
    loads[0].wait()
    for side in range(2):
        rows = pl.ds(0 if side == 0 else LR - 1, LS, stride=LR)
        for a in range(NV):
            for r in range(NRHS):
                pack_ref[0, side, a, r] = y0_ref[a, r, rows, :]
    send_halo(0, (2, 3))
    acc_ref[...] = jnp.zeros((NCOL, NCOL, 8, NT), jnp.float32)
    gram_block(y0_ref, y0_ref, acc_ref, 0, 0)
    loads[1].wait()
    def spread(round_index, value, slots, send, recv, count, me, peer):
        slots[round_index, me] = value
        copies = []
        for offset in range(1, count):
            copies.append(
                pltpu.make_async_remote_copy(
                    src_ref=slots.at[round_index, me],
                    dst_ref=slots.at[round_index, me],
                    send_sem=send.at[round_index, offset],
                    recv_sem=recv.at[round_index, offset],
                    device_id=peer(offset),
                    device_id_type=MESH,
                )
            )
        for copy in copies:
            copy.start()
        return copies

    def collect(round_index, copies, slots, count):
        for copy in copies:
            copy.wait()
        total = slots[round_index, 0]
        for index in range(1, count):
            total = total + slots[round_index, index]
        return total

    def start_first(index, value):
        return spread(
            index, value, first_ref, first_send, first_recv, n_first, me_first, first_peer
        )

    def start_second(index, copies):
        value = collect(index, copies, first_ref, n_first)
        return spread(
            index, value, second_ref, second_send, second_recv, n_second, chip, second_peer
        )

    pending = None
    for k in range(POWERS):
        scale = RAISE if k == 0 else 1.0
        target = ys[k + 1]
        for j in range(k + 1 if k else 0):
            gram_block(ys[k], ys[j], acc_ref, k, j)
        last = k == POWERS - 1
        if last:
            pending = start_first(0, gram_columns(acc_ref, range(DONE)))
        apply_inner(
            ys[k],
            target,
            diag_ref,
            face_ref,
            w_ref,
            stages,
            ahead_ref,
            open_ref,
            scale,
            diag_ready if k == 0 else None,
        )
        if last:
            pending = start_second(0, pending)
        wait_halo(k)
        add_halo(
            target,
            face_ref,
            halo_w_ref,
            (slab_ref[k, 0], slab_ref[k, 1]),
            (edge_ref[k, 0], edge_ref[k, 1]),
            None if last else pack_ref.at[k + 1],
            scale,
        )
        if not last:
            send_halo(k + 1, (2, 3, 0, 1))

    for j in range(POWERS + 1):
        gram_block(ys[POWERS], ys[j], acc_ref, POWERS, j)
    final = start_first(1, gram_columns(acc_ref, range(DONE, NCOL)))
    early = collect(0, pending, second_ref, n_second)
    work, across = eliminate(early, DONE)
    slice_out = combine(work, across, ys, c_ref, q_ref, range(DONE))

    def fill(t, carry):
        slice_out(t // FILL_STEPS, t % FILL_STEPS)
        return carry

    lax.fori_loop(0, FILL_STEPS, fill, 0)
    final = start_second(1, final)
    lax.fori_loop(FILL_STEPS, NV * FILL_STEPS, fill, 0)
    gram_ref[...] = early + collect(1, final, second_ref, n_second)
    for k in range(POWERS):
        for j in range(4):

            @pl.when(present[j])
            def _(k=k, j=j):
                halo_copy(k, j).wait_send()


def krylov(n_stream, n_radial, right, diag, face, jac):
    hbm = pl.BlockSpec(memory_space=pltpu.HBM)
    f32 = jnp.float32
    dma = pltpu.SemaphoreType.DMA
    n_first = 2 * n_radial
    n_second = n_stream // 2
    return pl.pallas_call(
        functools.partial(krylov_kernel, n_stream, n_radial),
        out_shape=(
            *[pltpu.VMEM((NV, NRHS, ROWS + LR, NT), f32)] * (POWERS + 1),
            pltpu.VMEM((NV, DONE, ROWS, NT), f32),
            pltpu.VMEM((NCOL, NT), f32),
        ),
        in_specs=[hbm] * 4,
        out_specs=tuple([pl.BlockSpec(memory_space=pltpu.VMEM)] * (POWERS + 3)),
        scratch_shapes=[
            pltpu.VMEM((NV, NV, ROWS, NT), f32),
            pltpu.VMEM((6, ROWS, NT), f32),
            pltpu.SMEM((NV, 6, NV), f32),
            pltpu.VMEM((6 * BLK, KDIM), jnp.bfloat16),
            pltpu.VMEM((4 * BLK, KDIM), jnp.bfloat16),
            pltpu.VMEM((NV, NRHS, LR, NT), f32),
            pltpu.VMEM((NV, NRHS, LR, NT), f32),
            pltpu.VMEM((NV, NRHS, LR, NT), f32),
            pltpu.VMEM((NV, NRHS, LR, NT), f32),
            pltpu.VMEM((NV, NRHS, LR, NT), f32),
            pltpu.VMEM((NV, NRHS, LR, NT), f32),
            pltpu.VMEM((POWERS, 2, NV, NRHS, LR, NT), f32),
            pltpu.VMEM((POWERS, 2, NV, NRHS, LS, NT), f32),
            pltpu.VMEM((POWERS, 2, NV, NRHS, LS, NT), f32),
            pltpu.VMEM((NCOL, NCOL, 8, NT), f32),
            pltpu.VMEM((NCOL, NCOL, NT), f32),
            pltpu.VMEM((2, n_first, NCOL, NT), f32),
            pltpu.VMEM((2, n_second, NCOL, NT), f32),
            dma((3 + LS // UNROLL,)),
            dma((POWERS, 4)),
            dma((POWERS, 4)),
            dma((2, n_first)),
            dma((2, n_first)),
            dma((2, n_second)),
            dma((2, n_second)),
        ],
        compiler_params=pltpu.CompilerParams(collective_id=0, has_side_effects=True, vmem_limit_bytes=47_600_000),
    )(right, diag, face, jac)


def basis_kernel(
    gram_ref, y0_ref, y1_ref, y2_ref, y3_ref, early_ref, q_hbm, r_ref, c_ref, late_ref, sem
):
    copies = [
        pltpu.make_async_copy(early_ref.at[a], q_hbm.at[a, pl.ds(0, DONE)], sem.at[0, a])
        for a in range(NV)
    ]
    for copy in copies:
        copy.start()
    work, across = eliminate(gram_ref[...], NCOL)
    row = lax.broadcasted_iota(jnp.int32, (NCOL, NT), 0)
    col = lax.broadcasted_iota(jnp.int32, (NCOL, NT), 1)
    r_ref[...] = jnp.where(row <= col, work, 0.0)[:, :NCOL]
    fields = (y0_ref, y1_ref, y2_ref, y3_ref)
    slice_out = combine(work, across, fields, c_ref, late_ref, range(DONE, NCOL))
    for a in range(NV):

        def fill(t, carry, a=a):
            slice_out(a, t)
            return carry

        lax.fori_loop(0, FILL_STEPS, fill, 0)
        copy = pltpu.make_async_copy(
            late_ref.at[a], q_hbm.at[a, pl.ds(DONE, NCOL - DONE)], sem.at[1, a]
        )
        copy.start()
        copies.append(copy)
    for copy in copies:
        copy.wait()


def basis(gram, early, fields):
    f32 = jnp.float32
    vmem = pl.BlockSpec(memory_space=pltpu.VMEM)
    return pl.pallas_call(
        basis_kernel,
        out_shape=(
            jax.ShapeDtypeStruct((NV, NCOL, ROWS, NT), f32),
            jax.ShapeDtypeStruct((NCOL, NCOL), f32),
        ),
        in_specs=[vmem] * (POWERS + 3),
        out_specs=(pl.BlockSpec(memory_space=pltpu.HBM), vmem),
        scratch_shapes=[
            pltpu.VMEM((NCOL, NCOL, NT), f32),
            pltpu.VMEM((NV, NCOL - DONE, ROWS, NT), f32),
            pltpu.SemaphoreType.DMA((2, NV)),
        ],
        compiler_params=pltpu.CompilerParams(vmem_limit_bytes=24 * 2**20),
    )(gram, *fields, early)


def body(n_stream, n_radial, right_side, diag_block, face_coef, jacobians):
    right = right_side.reshape(NV, NRHS, ROWS, NT)
    diag = diag_block.reshape(NV, NV, ROWS, NT)
    face = face_coef.reshape(6, ROWS, NT)
    jac = jnp.transpose(jacobians, (1, 0, 2))
    *fields, early, gram = krylov(n_stream, n_radial, right, diag, face, jac)
    q, r_factor = basis(gram, early, fields)
    return q.reshape(NV, NCOL, LS, LR, NT), r_factor


def solution(mesh):
    return jax.shard_map(
        functools.partial(body, mesh.shape["stream"], mesh.shape["radial"]),
        mesh=mesh,
        in_specs=(
            P(None, None, "stream", "radial", None),
            P(None, None, "stream", "radial", None),
            P(None, "stream", "radial", None),
            P(),
        ),
        out_specs=(P(None, None, "stream", "radial", None), P()),
        check_vma=False,
    )
```

```python
import functools

import jax
import jax.numpy as jnp
from jax import lax
from jax.experimental import pallas as pl
from jax.experimental.pallas import tpu as pltpu
from jax.sharding import PartitionSpec as P

NV = 5
NRHS = 4
POWERS = 3
NCOL = 16
LS = 16
LR = 16
NT = 128
ROWS = LS * LR
SHIFT = 6.0
BLK = NV * LR
KDIM = 256
OFFSETS = (0, 0, -1, 1, 0, 0)
UNROLL = 4
DIAG_ROWS = UNROLL * LR
GRAM_ROWS = 16
GRAM_UNROLL = 8
GRAM_STEPS = ROWS // (GRAM_ROWS * GRAM_UNROLL)
FILL_ROWS = 32
FILL_UNROLL = 2
FILL_STEPS = ROWS // (FILL_ROWS * FILL_UNROLL)
DONE = 12
RAISE = 2.0**24
MESH = pl.DeviceIdType.MESH


def build_operator(jac_ref, w_ref, halo_w_ref):
    col = lax.broadcasted_iota(jnp.int32, (LR, KDIM), 1)
    row = lax.broadcasted_iota(jnp.int32, (LR, KDIM), 0)
    part = col // BLK
    var = (col % BLK) // LR
    cell = col % LR
    masks = {}
    for offset in (-1, 0, 1):
        hit = (cell == row + offset) & (part < 3)
        masks[offset] = [
            jnp.where(hit & (var == b), -1.0, 0.0).astype(jnp.float32) for b in range(NV)
        ]

    def tile(direction, a, offset):
        total = jac_ref[a, direction, 0] * masks[offset][0]
        for b in range(1, NV):
            total = total + jac_ref[a, direction, b] * masks[offset][b]
        head = total.astype(jnp.bfloat16).astype(jnp.float32)
        return jnp.where(part == 1, total - head, head).astype(jnp.bfloat16)

    for a in range(NV):
        for direction, offset in enumerate(OFFSETS):
            start = (a * 6 + direction) * LR
            w_ref[start : start + LR, :] = tile(direction, a, offset)
        for direction in range(4):
            start = direction * BLK + a * LR
            halo_w_ref[start : start + LR, :] = tile(direction, a, 0)


def split_fields(values):
    head = values.astype(jnp.bfloat16)
    tail = (values - head.astype(jnp.float32)).astype(jnp.bfloat16)
    empty = jnp.zeros((KDIM - 3 * BLK, NT), jnp.bfloat16)
    columns = []
    for r in range(NRHS):
        head_r = head[:, r].reshape(BLK, NT)
        tail_r = tail[:, r].reshape(BLK, NT)
        columns.append(jnp.concatenate([head_r, head_r, tail_r, empty], axis=0))
    return jnp.concatenate(columns, axis=1)


def slab(s):
    return pl.ds(pl.multiple_of(s * LR, LR), LR)


def apply_blocks(source, diag_ref, stage, s, scale):
    for half in range(2):
        rows = pl.ds(pl.multiple_of(s * LR + half * 8, 8), 8)
        fields = [[source[b, r, rows, :] for r in range(NRHS)] for b in range(NV)]
        for a in range(NV):
            totals = [None] * NRHS
            for b in range(NV):
                block = diag_ref[a, b, rows, :]
                if scale != 1.0:
                    block = block * scale
                for r in range(NRHS):
                    term = block * fields[b][r]
                    totals[r] = term if b == 0 else totals[r] + term
            for r in range(NRHS):
                stage[a, r, half * 8 : half * 8 + 8, :] = totals[r]


def apply_inner(
    source, target, diag_ref, face_ref, w_ref, stages, ahead_ref, open_ref, scale, prepare=None
):
    cells = [(a, r) for a in range(NV) for r in range(NRHS)]
    ahead_ref[...] = jnp.zeros((NV, NRHS, LR, NT), jnp.float32)
    open_ref[...] = jnp.zeros((NV, NRHS, LR, NT), jnp.float32)

    def step(t, carry):
        s0 = t * UNROLL
        if prepare is not None:
            prepare(t)
        for u in range(UNROLL):
            apply_blocks(source, diag_ref, stages[u], s0 + u, scale)
        ahead = {cell: ahead_ref[cell[0], cell[1]] for cell in cells}
        unfinished = {cell: open_ref[cell[0], cell[1]] for cell in cells}
        for u in range(UNROLL):
            s = s0 + u
            before = jnp.where(s == 0, LS, s - 1) if u == 0 else s - 1
            product = jnp.dot(
                w_ref[...],
                split_fields(source[:, :, slab(s), :]),
                preferred_element_type=jnp.float32,
            )
            face = [face_ref[0, slab(jnp.minimum(s + 1, LS - 1)), :]]
            face.append(face_ref[1, slab(jnp.maximum(s - 1, 0)), :])
            face += [face_ref[d, slab(s), :] for d in range(2, 6)]
            if scale != 1.0:
                face = [weight * scale for weight in face]
            for a, r in cells:

                def part(d, a=a, r=r):
                    start = (a * 6 + d) * LR
                    return product[start : start + LR, r * NT : (r + 1) * NT]

                target[a, r, slab(before), :] = unfinished[a, r] + face[1] * part(1)
                total = face[2] * part(2) + face[3] * part(3)
                total = total + face[4] * pltpu.roll(part(4), 1, 1)
                total = total + face[5] * pltpu.roll(part(5), NT - 1, 1)
                unfinished[a, r] = total + (stages[u][a, r] + ahead[a, r])
                ahead[a, r] = face[0] * part(0)
        for a, r in cells:
            ahead_ref[a, r] = ahead[a, r]
            open_ref[a, r] = unfinished[a, r]
        return carry

    lax.fori_loop(0, LS // UNROLL, step, 0)
    target[:, :, ROWS - LR : ROWS, :] = open_ref[...]


def add_halo(target, face_ref, halo_w_ref, slabs, edges, rows_ref, scale, arrive, leave):
    arrive((0, 1))
    for side in range(2):
        start = 0 if side == 0 else ROWS - LR
        product = jnp.dot(
            halo_w_ref[side * BLK : (side + 1) * BLK, :],
            split_fields(slabs[side][...]),
            preferred_element_type=jnp.float32,
        )
        weight = face_ref[side, start : start + LR, :] * scale
        for a in range(NV):
            for r in range(NRHS):
                target[a, r, start : start + LR, :] = target[a, r, start : start + LR, :] + (
                    weight * product[a * LR : (a + 1) * LR, r * NT : (r + 1) * NT]
                )
    for side in range(2):
        arrive((2 + side,))
        rows = pl.ds(0 if side == 0 else LR - 1, LS, stride=LR)
        product = jnp.dot(
            halo_w_ref[(2 + side) * BLK : (3 + side) * BLK, :],
            split_fields(edges[side][...]),
            preferred_element_type=jnp.float32,
        )
        weight = face_ref[2 + side, rows, :] * scale
        for a in range(NV):
            for r in range(NRHS):
                fresh = target[a, r, rows, :] + weight * (
                    product[a * LR : (a + 1) * LR, r * NT : (r + 1) * NT]
                )
                target[a, r, rows, :] = fresh
                if rows_ref is not None:
                    rows_ref[side, a, r] = fresh
        leave((3 - side,))
    leave((0, 1))


def gram_block(left, right, acc_ref, k, j):
    pairs = [(p, q) for p in range(NRHS) for q in range(NRHS) if k != j or q <= p]

    def step(t, sums):
        a = t // GRAM_STEPS
        sums = list(sums)
        for u in range(GRAM_UNROLL):
            start = ((t % GRAM_STEPS) * GRAM_UNROLL + u) * GRAM_ROWS
            rows = pl.ds(pl.multiple_of(start, GRAM_ROWS), GRAM_ROWS)
            mine = [left[a, p, rows, :] for p in range(NRHS)]
            other = mine if k == j else [right[a, q, rows, :] for q in range(NRHS)]
            for index, (p, q) in enumerate(pairs):
                term = mine[p] * other[q]
                for piece in range(GRAM_ROWS // 8):
                    sums[index] = sums[index] + term[piece * 8 : piece * 8 + 8]
        return tuple(sums)

    empty = tuple(jnp.zeros((8, NT), jnp.float32) for _ in pairs)
    sums = lax.fori_loop(0, NV * GRAM_STEPS, step, empty)
    for index, (p, q) in enumerate(pairs):
        acc_ref[4 * k + p, 4 * j + q] = sums[index]
        if k == j and p != q:
            acc_ref[4 * k + q, 4 * j + p] = sums[index]


def gram_columns(acc_ref, columns):
    lane = lax.broadcasted_iota(jnp.int32, (NCOL, NT), 1)
    table = jnp.zeros((NCOL, NT), jnp.float32)
    for i in columns:
        rows = jnp.sum(acc_ref[i], axis=1)
        table = table + jnp.where(lane == i, jnp.sum(rows, axis=1, keepdims=True), 0.0)
    return table


def eliminate(table, count):
    row = lax.broadcasted_iota(jnp.int32, (NCOL, NT), 0)
    col = lax.broadcasted_iota(jnp.int32, (NCOL, NT), 1)
    square = table[:, :NCOL]
    flipped = jnp.concatenate([square.T, jnp.zeros((NCOL, NT - NCOL), jnp.float32)], axis=1)
    gram = jnp.where((row // NRHS > col // NRHS) & (col < NCOL), flipped, table)
    on_diag = jnp.where(row == col, gram, 0.0)
    down = jnp.sum(on_diag, axis=1, keepdims=True)
    across = jnp.sum(on_diag, axis=0, keepdims=True)
    down = 1.0 / jnp.sqrt(jnp.where(row[:, :1] < count, down, 1.0))
    across = 1.0 / jnp.sqrt(jnp.where(col[:1] < count, across, 1.0))
    work = gram * down * across
    work = jnp.where(col == row + NCOL, 1.0, work)
    for i in range(count):
        line = work[i : i + 1, :] * (1.0 / work[i : i + 1, i : i + 1])
        work = jnp.where(row > i, work - work[:, i : i + 1] * line, work)
    pivots = jnp.sum(jnp.where(row == col, work, 0.0), axis=1, keepdims=True)
    work = work * (1.0 / jnp.sqrt(jnp.where(row[:, :1] < count, pivots, 1.0)))
    return work, across


def combine(work, across, fields, c_ref, out_ref, columns):
    last = columns[-1] + 1
    for i in range(last):
        lifted = work[:, NCOL + i : NCOL + i + 1] * across[:, i : i + 1]
        c_ref[i] = jnp.broadcast_to(lifted, (NCOL, NT))

    def slice_out(a, t):
        for u in range(FILL_UNROLL):
            part_out(a, (t * FILL_UNROLL + u) * FILL_ROWS)

    def part_out(a, start):
        here = pl.ds(pl.multiple_of(start, FILL_ROWS), FILL_ROWS)
        values = [fields[i // NRHS][a, i % NRHS, here, :] for i in range(last)]
        for j in columns:
            total = c_ref[0, j : j + 1, :] * values[0]
            for i in range(1, j + 1):
                total = total + c_ref[i, j : j + 1, :] * values[i]
            out_ref[a, j - columns[0], here, :] = total

    return slice_out


def krylov_kernel(
    n_stream,
    n_radial,
    right_hbm,
    diag_hbm,
    face_hbm,
    jac_hbm,
    y0_ref,
    y1_ref,
    y2_ref,
    y3_ref,
    q_ref,
    gram_ref,
    diag_ref,
    face_ref,
    jac_ref,
    w_ref,
    halo_w_ref,
    stage0_ref,
    stage1_ref,
    stage2_ref,
    stage3_ref,
    ahead_ref,
    open_ref,
    slab_ref,
    edge_ref,
    pack_ref,
    acc_ref,
    c_ref,
    first_ref,
    second_ref,
    load_sem,
    halo_send,
    halo_recv,
    first_send,
    first_recv,
    second_send,
    second_recv,
):
    ys = (y0_ref, y1_ref, y2_ref, y3_ref)
    stages = (stage0_ref, stage1_ref, stage2_ref, stage3_ref)
    si = lax.axis_index("stream")
    ri = lax.axis_index("radial")
    core = si % 2
    chip = si // 2
    n_first = 2 * n_radial
    n_second = n_stream // 2
    me_first = ri * 2 + core

    def first_peer(offset):
        other = (me_first + offset) % n_first
        return (chip * 2 + other % 2, other // 2)

    def second_peer(offset):
        return (((chip + offset) % n_second) * 2 + core, ri)

    loads = [
        pltpu.make_async_copy(right_hbm, y0_ref.at[:, :, pl.ds(0, ROWS), :], load_sem.at[0]),
        pltpu.make_async_copy(face_hbm, face_ref, load_sem.at[1]),
        pltpu.make_async_copy(jac_hbm, jac_ref, load_sem.at[2]),
    ]

    def diag_load(t):
        rows = pl.ds(pl.multiple_of(t * DIAG_ROWS, DIAG_ROWS), DIAG_ROWS)
        return pltpu.make_async_copy(
            diag_hbm.at[:, :, rows, :], diag_ref.at[:, :, rows, :], load_sem.at[3 + t]
        )

    def diag_ready(t):
        rows = pl.ds(pl.multiple_of(t * DIAG_ROWS, DIAG_ROWS), DIAG_ROWS)
        diag_load(t).wait()
        for a in range(NV):
            diag_ref[a, a, rows, :] = diag_ref[a, a, rows, :] - SHIFT

    loads[2].start()
    loads[0].start()
    loads[1].start()
    for t in range(LS // UNROLL):
        diag_load(t).start()

    barrier = pltpu.get_barrier_semaphore()
    peers = ((si + 1, ri), (si - 1, ri), (si, ri + 1), (si, ri - 1))
    present = (si < n_stream - 1, si > 0, ri < n_radial - 1, ri > 0)
    source_of = (1, 0, 3, 2)
    for j in range(4):

        @pl.when(present[j])
        def _(j=j):
            pl.semaphore_signal(barrier, inc=1, device_id=peers[j], device_id_type=MESH)

    for offset in range(1, n_first):
        pl.semaphore_signal(barrier, inc=1, device_id=first_peer(offset), device_id_type=MESH)
    for offset in range(1, n_second):
        pl.semaphore_signal(barrier, inc=1, device_id=second_peer(offset), device_id_type=MESH)
    loads[2].wait()
    build_operator(jac_ref, w_ref, halo_w_ref)
    for side in range(2):

        @pl.when(jnp.logical_not(present[1 - side]))
        def _(side=side):
            slab_ref[:, side] = jnp.zeros((POWERS, NV, NRHS, LR, NT), jnp.float32)

        @pl.when(jnp.logical_not(present[3 - side]))
        def _(side=side):
            edge_ref[:, side] = jnp.zeros((POWERS, NV, NRHS, LS, NT), jnp.float32)

    greeted = n_first - 1 + n_second - 1
    for j in range(4):
        greeted = greeted + present[j].astype(jnp.int32)
    pl.semaphore_wait(barrier, greeted)

    def halo_copy(k, j):
        if j < 2:
            start = ROWS - LR if j == 0 else 0
            whole = right_hbm if k == 0 else ys[k]
            src = whole.at[:, :, pl.ds(start, LR), :]
            dst = slab_ref.at[k, j]
        else:
            src = pack_ref.at[k, 3 - j]
            dst = edge_ref.at[k, j - 2]
        return pltpu.make_async_remote_copy(
            src_ref=src,
            dst_ref=dst,
            send_sem=halo_send.at[k, j],
            recv_sem=halo_recv.at[k, j],
            device_id=peers[j],
            device_id_type=MESH,
        )

    def send_halo(k, js):
        for j in js:

            @pl.when(present[j])
            def _(j=j):
                halo_copy(k, j).start()

    def wait_halo(k, js):
        for j in js:

            @pl.when(present[source_of[j]])
            def _(j=j):
                halo_copy(k, j).wait_recv()

    send_halo(0, (0, 1))
    loads[0].wait()
    for side in range(2):
        rows = pl.ds(0 if side == 0 else LR - 1, LS, stride=LR)
        for a in range(NV):
            for r in range(NRHS):
                pack_ref[0, side, a, r] = y0_ref[a, r, rows, :]
    send_halo(0, (2, 3))
    acc_ref[...] = jnp.zeros((NCOL, NCOL, 8, NT), jnp.float32)
    gram_block(y0_ref, y0_ref, acc_ref, 0, 0)
    loads[1].wait()
    def spread(round_index, value, slots, send, recv, count, me, peer):
        slots[round_index, me] = value
        copies = []
        for offset in range(1, count):
            copies.append(
                pltpu.make_async_remote_copy(
                    src_ref=slots.at[round_index, me],
                    dst_ref=slots.at[round_index, me],
                    send_sem=send.at[round_index, offset],
                    recv_sem=recv.at[round_index, offset],
                    device_id=peer(offset),
                    device_id_type=MESH,
                )
            )
        for copy in copies:
            copy.start()
        return copies

    def collect(round_index, copies, slots, count):
        for copy in copies:
            copy.wait()
        total = slots[round_index, 0]
        for index in range(1, count):
            total = total + slots[round_index, index]
        return total

    def start_first(index, value):
        return spread(
            index, value, first_ref, first_send, first_recv, n_first, me_first, first_peer
        )

    def start_second(index, copies):
        value = collect(index, copies, first_ref, n_first)
        return spread(
            index, value, second_ref, second_send, second_recv, n_second, chip, second_peer
        )

    pending = None
    for k in range(POWERS):
        scale = RAISE if k == 0 else 1.0
        target = ys[k + 1]
        for j in range(k + 1 if k else 0):
            gram_block(ys[k], ys[j], acc_ref, k, j)
        last = k == POWERS - 1
        if last:
            pending = start_first(0, gram_columns(acc_ref, range(DONE)))
        apply_inner(
            ys[k],
            target,
            diag_ref,
            face_ref,
            w_ref,
            stages,
            ahead_ref,
            open_ref,
            scale,
            diag_ready if k == 0 else None,
        )
        if last:
            pending = start_second(0, pending)
        add_halo(
            target,
            face_ref,
            halo_w_ref,
            (slab_ref.at[k, 0], slab_ref.at[k, 1]),
            (edge_ref.at[k, 0], edge_ref.at[k, 1]),
            None if last else pack_ref.at[k + 1],
            scale,
            functools.partial(wait_halo, k),
            (lambda js: None) if last else functools.partial(send_halo, k + 1),
        )

    for j in range(POWERS + 1):
        gram_block(ys[POWERS], ys[j], acc_ref, POWERS, j)
    final = start_first(1, gram_columns(acc_ref, range(DONE, NCOL)))
    early = collect(0, pending, second_ref, n_second)
    work, across = eliminate(early, DONE)
    slice_out = combine(work, across, ys, c_ref, q_ref, range(DONE))

    def fill(t, carry):
        slice_out(t // FILL_STEPS, t % FILL_STEPS)
        return carry

    lax.fori_loop(0, FILL_STEPS, fill, 0)
    final = start_second(1, final)
    lax.fori_loop(FILL_STEPS, NV * FILL_STEPS, fill, 0)
    gram_ref[...] = early + collect(1, final, second_ref, n_second)
    for k in range(POWERS):
        for j in range(4):

            @pl.when(present[j])
            def _(k=k, j=j):
                halo_copy(k, j).wait_send()


def krylov(n_stream, n_radial, right, diag, face, jac):
    hbm = pl.BlockSpec(memory_space=pltpu.HBM)
    f32 = jnp.float32
    dma = pltpu.SemaphoreType.DMA
    n_first = 2 * n_radial
    n_second = n_stream // 2
    return pl.pallas_call(
        functools.partial(krylov_kernel, n_stream, n_radial),
        out_shape=(
            *[pltpu.VMEM((NV, NRHS, ROWS + LR, NT), f32)] * (POWERS + 1),
            pltpu.VMEM((NV, DONE, ROWS, NT), f32),
            pltpu.VMEM((NCOL, NT), f32),
        ),
        in_specs=[hbm] * 4,
        out_specs=tuple([pl.BlockSpec(memory_space=pltpu.VMEM)] * (POWERS + 3)),
        scratch_shapes=[
            pltpu.VMEM((NV, NV, ROWS, NT), f32),
            pltpu.VMEM((6, ROWS, NT), f32),
            pltpu.SMEM((NV, 6, NV), f32),
            pltpu.VMEM((6 * BLK, KDIM), jnp.bfloat16),
            pltpu.VMEM((4 * BLK, KDIM), jnp.bfloat16),
            pltpu.VMEM((NV, NRHS, LR, NT), f32),
            pltpu.VMEM((NV, NRHS, LR, NT), f32),
            pltpu.VMEM((NV, NRHS, LR, NT), f32),
            pltpu.VMEM((NV, NRHS, LR, NT), f32),
            pltpu.VMEM((NV, NRHS, LR, NT), f32),
            pltpu.VMEM((NV, NRHS, LR, NT), f32),
            pltpu.VMEM((POWERS, 2, NV, NRHS, LR, NT), f32),
            pltpu.VMEM((POWERS, 2, NV, NRHS, LS, NT), f32),
            pltpu.VMEM((POWERS, 2, NV, NRHS, LS, NT), f32),
            pltpu.VMEM((NCOL, NCOL, 8, NT), f32),
            pltpu.VMEM((NCOL, NCOL, NT), f32),
            pltpu.VMEM((2, n_first, NCOL, NT), f32),
            pltpu.VMEM((2, n_second, NCOL, NT), f32),
            dma((3 + LS // UNROLL,)),
            dma((POWERS, 4)),
            dma((POWERS, 4)),
            dma((2, n_first)),
            dma((2, n_first)),
            dma((2, n_second)),
            dma((2, n_second)),
        ],
        compiler_params=pltpu.CompilerParams(collective_id=0, has_side_effects=True, vmem_limit_bytes=47_600_000),
    )(right, diag, face, jac)


def basis_kernel(
    gram_ref, y0_ref, y1_ref, y2_ref, y3_ref, early_ref, q_hbm, r_ref, c_ref, late_ref, sem
):
    copies = [
        pltpu.make_async_copy(early_ref.at[a], q_hbm.at[a, pl.ds(0, DONE)], sem.at[0, a])
        for a in range(NV)
    ]
    for copy in copies:
        copy.start()
    work, across = eliminate(gram_ref[...], NCOL)
    row = lax.broadcasted_iota(jnp.int32, (NCOL, NT), 0)
    col = lax.broadcasted_iota(jnp.int32, (NCOL, NT), 1)
    r_ref[...] = jnp.where(row <= col, work, 0.0)[:, :NCOL]
    fields = (y0_ref, y1_ref, y2_ref, y3_ref)
    slice_out = combine(work, across, fields, c_ref, late_ref, range(DONE, NCOL))
    for a in range(NV):

        def fill(t, carry, a=a):
            slice_out(a, t)
            return carry

        lax.fori_loop(0, FILL_STEPS, fill, 0)
        copy = pltpu.make_async_copy(
            late_ref.at[a], q_hbm.at[a, pl.ds(DONE, NCOL - DONE)], sem.at[1, a]
        )
        copy.start()
        copies.append(copy)
    for copy in copies:
        copy.wait()


def basis(gram, early, fields):
    f32 = jnp.float32
    vmem = pl.BlockSpec(memory_space=pltpu.VMEM)
    return pl.pallas_call(
        basis_kernel,
        out_shape=(
            jax.ShapeDtypeStruct((NV, NCOL, ROWS, NT), f32),
            jax.ShapeDtypeStruct((NCOL, NCOL), f32),
        ),
        in_specs=[vmem] * (POWERS + 3),
        out_specs=(pl.BlockSpec(memory_space=pltpu.HBM), vmem),
        scratch_shapes=[
            pltpu.VMEM((NCOL, NCOL, NT), f32),
            pltpu.VMEM((NV, NCOL - DONE, ROWS, NT), f32),
            pltpu.SemaphoreType.DMA((2, NV)),
        ],
        compiler_params=pltpu.CompilerParams(vmem_limit_bytes=24 * 2**20),
    )(gram, *fields, early)


def body(n_stream, n_radial, right_side, diag_block, face_coef, jacobians):
    right = right_side.reshape(NV, NRHS, ROWS, NT)
    diag = diag_block.reshape(NV, NV, ROWS, NT)
    face = face_coef.reshape(6, ROWS, NT)
    jac = jnp.transpose(jacobians, (1, 0, 2))
    *fields, early, gram = krylov(n_stream, n_radial, right, diag, face, jac)
    q, r_factor = basis(gram, early, fields)
    return q.reshape(NV, NCOL, LS, LR, NT), r_factor


def solution(mesh):
    return jax.shard_map(
        functools.partial(body, mesh.shape["stream"], mesh.shape["radial"]),
        mesh=mesh,
        in_specs=(
            P(None, None, "stream", "radial", None),
            P(None, None, "stream", "radial", None),
            P(None, "stream", "radial", None),
            P(),
        ),
        out_specs=(P(None, None, "stream", "radial", None), P()),
        check_vma=False,
    )
```
